512 devices in a mesh: dp: 64 (over z, x), feat: 8 (over y, core).
Axes of the slice: x: 4, y: 4, z: 16, core: 2. Of those that a mesh axis runs over, the one named last changes fastest.
Arguments:
- teacher: bfloat16 [8192, 1024], P('dp'), may hold values from -6 to 6
- student: bfloat16 [8192, 768], P('dp'), may hold values from -6 to 6
- head: bfloat16 [768, 1024], P(None, 'feat'), may hold values from -0.21875 to 0.21875
- freqs: bfloat16 [1024, 2048], P(None, 'feat'), may hold values from -0.1875 to 0.1875
- labels: int32 [8192], P('dp'), may hold values from 0 to 21823, as said below
- class_slot: int32 [21824], replicated, may hold values from 0 to 21823, as said below
Outputs:
- head_grad: float32 [1024, 768], P(('dp', 'feat'))
- class_loss: float32 [21824], P('dp')
The draws below stay inside these ranges and needn't reach their ends.
Inputs may be any that keep to these rules, and one draw needn't show every extreme that they name: class_slot is a permutation of the classes. Of the 128 labels of one dp index, at most 4 have class_slot[label] // 341 equal to any one dp index; for one dp index that bound is reached from every dp index.
All inputs are finite; a program needn't handle non-finite values.
Results may differ from the reference program's by a relative error of at most 0.005.
Values may be sent and summed in bfloat16 or wider, within the bound.
A program may use at most 64 MiB of HBM per device.

```python
import jax
import jax.numpy as jnp
from jax import lax

D_T = 1024
D_S = 768
FREQ = 2048
CLS_DEV = 341
IMG_DEV = 128
CAP = 4
IMAGES = 8192
CLASSES = 21824


def slot_table(key):
    return jax.random.permutation(jax.random.fold_in(key, 11), CLASSES).astype(jnp.int32)


def draw_class_slot(key, part):
    return slot_table(key)


def draw_labels(key, part):
    groups = IMAGES // IMG_DEV
    table = slot_table(key)
    inverse = jnp.zeros((CLASSES,), jnp.int32).at[table].set(jnp.arange(CLASSES, dtype=jnp.int32))
    hottest = jax.random.randint(jax.random.fold_in(key, 12), (), 0, groups).astype(jnp.int32)

    def one_group(group_key):
        keys = jax.random.split(group_key, 4)
        spare = jax.random.permutation(keys[0], (groups - 1) * CAP).astype(jnp.int32)[:IMG_DEV - CAP]
        others = spare // CAP
        others = jnp.where(others >= hottest, others + 1, others)
        owners = jnp.concatenate([jnp.full((CAP,), hottest, jnp.int32), others])
        order = jax.random.permutation(keys[1], IMG_DEV).astype(jnp.int32)
        owners = owners[order]
        first = jax.random.randint(keys[2], (IMG_DEV,), 0, CLS_DEV).astype(jnp.int32)
        second = jax.random.randint(keys[3], (IMG_DEV,), 0, CLS_DEV).astype(jnp.int32)
        local = first * second // CLS_DEV
        return inverse[owners * CLS_DEV + local]
    group_keys = jax.random.split(jax.random.fold_in(key, 13), groups)
    return jax.vmap(one_group)(group_keys).reshape(IMAGES)


def shard_levels(rng, extent, cuts, least, top_value):
    level = 1.0
    for position, parts in cuts:
        heights = jax.random.uniform(jax.random.fold_in(jax.random.fold_in(rng, 6), position), (parts,), jnp.float32, least / len(cuts), top_value / len(cuts))
        level = level * jnp.repeat(jnp.exp(heights), extent[position] // parts).reshape((-1,) + (1,) * (len(extent) - 1 - position))
    return level


def normal_values(own_key, dims, spread, most, cuts=(), kind=jnp.bfloat16):
    factor_of = shard_levels(own_key, dims, cuts, -0.22, 0.18) if cuts else 1.0
    drawn = jax.random.normal(own_key, dims, jnp.float32) * spread * factor_of
    return jnp.minimum(jnp.maximum(drawn, -most), most).astype(kind)


def setup_inputs(seed: int = 0) -> dict:
    seeds = jax.random.split(jax.random.key(seed), 7)
    return {
        "teacher": normal_values(seeds[0], (IMAGES, D_T), 1.0, 6.0, ((0, 64),)),
        "student": normal_values(seeds[1], (IMAGES, D_S), 1.0, 6.0, ((0, 64),)),
        "head": normal_values(seeds[2], (D_S, D_T), D_S ** -0.5, 0.21875, ((1, 8),)),
        "freqs": normal_values(seeds[3], (D_T, FREQ), D_T ** -0.5, 0.1875, ((1, 8),)),
        "labels": draw_labels(jax.random.fold_in(seeds[6], 71), 0),
        "class_slot": draw_class_slot(jax.random.fold_in(seeds[6], 71), 0),
    }


def reference(teacher, student, head, freqs, labels, class_slot):
    projected = jnp.dot(student, head, preferred_element_type=jnp.float32).astype(jnp.bfloat16)
    student_z = jnp.dot(projected, freqs, preferred_element_type=jnp.float32)
    teacher_z = jnp.dot(teacher, freqs, preferred_element_type=jnp.float32)
    delta = jnp.concatenate([jnp.cos(student_z) - jnp.cos(teacher_z), jnp.sin(student_z) - jnp.sin(teacher_z)], axis=1)
    sums = jax.ops.segment_sum(delta, labels, num_segments=CLASSES)
    counts = jax.ops.segment_sum(jnp.ones(labels.shape, jnp.float32), labels, num_segments=CLASSES)
    floor_counts = jnp.maximum(counts, 1.0)
    means = sums / floor_counts[:, None]
    per_class = lax.optimization_barrier(jnp.sum(sums * sums, axis=1)) / floor_counts / (2.0 * FREQ)
    class_loss = jnp.zeros((CLASSES,), jnp.float32).at[class_slot].set(per_class)
    picked = jnp.take(means, labels, axis=0)
    grad_z = (-jnp.sin(student_z) * picked[:, :FREQ] + jnp.cos(student_z) * picked[:, FREQ:]).astype(jnp.bfloat16)
    grad_u = jnp.dot(grad_z, freqs.T, preferred_element_type=jnp.float32)
    head_grad = jnp.dot(grad_u.T, student.astype(jnp.float32), precision=lax.Precision.HIGHEST)
    head_grad = head_grad / jnp.sqrt(jnp.float32(IMAGES))
    return (head_grad, class_loss)
```

```python
import math

import jax
import jax.numpy as jnp
from jax import lax
from jax.sharding import PartitionSpec as P


def split_parts(values):
    upper = values.astype(jnp.bfloat16)
    lower = (values - upper.astype(jnp.float32)).astype(jnp.bfloat16)
    return (upper, lower)


def dot(a, b, ca=1, cb=0):
    return lax.dot_general(a, b, (((ca,), (cb,)), ((), ())), preferred_element_type=jnp.float32)


def on_device(teacher, student, head, freqs, labels, class_slot):
    n_dp = lax.axis_size("dp")
    n_feat = lax.axis_size("feat")
    f = lax.axis_index("feat")
    images = labels.shape[0]
    half = freqs.shape[1]
    d_t = teacher.shape[1]
    d_s = student.shape[1]
    cls_dev = class_slot.shape[0] // n_dp
    capacity = 2 * images // n_dp
    slots = n_dp * capacity
    part = d_t // n_feat

    position = jnp.take(class_slot, labels)
    owner = position // cls_dev
    local_cls = position % cls_dev
    same = owner[:, None] == owner[None, :]
    before = jnp.arange(images)[:, None] > jnp.arange(images)[None, :]
    rank = jnp.sum((same & before).astype(jnp.int32), axis=1)
    slot = owner * capacity + rank
    select = (jnp.arange(slots, dtype=jnp.int32)[:, None] == slot[None, :]).astype(jnp.bfloat16)

    projected = dot(student, head).astype(jnp.bfloat16)
    tag = local_cls + 1
    lane = jnp.arange(part * n_feat - d_s, dtype=jnp.int32)[None, :]
    tags = jnp.where(lane == 0, (tag // 32)[:, None], jnp.where(lane == 1, (tag % 32)[:, None], 0))
    wide = jnp.concatenate([student, tags.astype(jnp.bfloat16)], axis=1)
    rows = jnp.concatenate(
        [
            lax.dynamic_slice_in_dim(teacher, f * part, part, axis=1),
            projected,
            lax.dynamic_slice_in_dim(wide, f * part, part, axis=1),
        ],
        axis=1,
    )
    outgoing = dot(select, rows).astype(jnp.bfloat16).reshape(n_dp, capacity, 3 * part)
    incoming = lax.all_to_all(outgoing, "dp", split_axis=0, concat_axis=0, tiled=True)
    incoming = incoming.reshape(slots, 3, part)
    full = lax.all_gather(incoming, "feat", axis=0, tiled=False)
    full = full.transpose(2, 1, 0, 3).reshape(3, slots, n_feat * part)
    teacher_in, projected_in, wide_in = full[0], full[1], full[2]
    student_in = wide_in[:, :d_s]
    tag_in = wide_in[:, d_s : d_s + 2].astype(jnp.int32)
    tag_in = tag_in[:, 0] * 32 + tag_in[:, 1]

    student_z = dot(projected_in, freqs)
    teacher_z = dot(teacher_in, freqs)
    cos_s, sin_s = jnp.cos(student_z), jnp.sin(student_z)
    delta = jnp.concatenate([cos_s - jnp.cos(teacher_z), sin_s - jnp.sin(teacher_z)], axis=1)
    alike = (tag_in[:, None] == tag_in[None, :]) & (tag_in[:, None] > 0)
    count = jnp.maximum(jnp.sum(alike.astype(jnp.float32), axis=1), 1.0)
    upper, lower = split_parts(delta)
    member = alike.astype(jnp.bfloat16)
    sums = dot(member, upper) + dot(member, lower)
    picked = sums / count[:, None]
    grad_z = (-sin_s * picked[:, :half] + cos_s * picked[:, half:]).astype(jnp.bfloat16)

    norm = jnp.sum(sums * sums, axis=1) / count
    holds = (jnp.arange(cls_dev, dtype=jnp.int32)[:, None] + 1) == tag_in[None, :]
    per_class = jnp.sum(jnp.where(holds, norm[None, :], 0.0), axis=1)
    counts = jnp.maximum(jnp.sum(holds.astype(jnp.float32), axis=1), 1.0)
    class_loss = lax.psum(per_class, "feat") / counts / (2.0 * half * n_feat)

    rows_dev = d_t // (n_dp * n_feat)
    freq_rows = lax.all_to_all(
        freqs.reshape(n_dp, n_feat, rows_dev, half), "feat", split_axis=1, concat_axis=3, tiled=True
    ).reshape(n_dp * rows_dev, half * n_feat)
    grad_z_full = lax.all_gather(grad_z, "feat", axis=1, tiled=True)
    grad_u = dot(grad_z_full, freq_rows, 1, 1)
    u_upper, u_lower = split_parts(grad_u)
    partial = dot(u_upper, student_in, 0, 0) + dot(u_lower, student_in, 0, 0)
    partial = partial.reshape(n_dp, rows_dev, d_s)
    parts = lax.all_to_all(partial.astype(jnp.bfloat16), "dp", split_axis=0, concat_axis=0, tiled=True)
    scale = 1.0 / math.sqrt(images * n_dp)
    head_grad = jnp.sum(parts.astype(jnp.float32), axis=0) * scale
    return (head_grad, class_loss)


def solution(mesh):
    in_specs = (P("dp", None), P("dp", None), P(None, "feat"), P(None, "feat"), P("dp"), P())
    out_specs = (P(("dp", "feat"), None), P("dp"))
    return jax.shard_map(
        on_device, mesh=mesh, in_specs=in_specs, out_specs=out_specs, check_vma=False
    )
```

```python
import functools
import math

import jax
import jax.numpy as jnp
from jax import lax
from jax.experimental import pallas as pl
from jax.experimental.pallas import tpu as pltpu
from jax.sharding import PartitionSpec as P

F32, BF16 = jnp.float32, jnp.bfloat16
NX, NC = 4, 2
COPIES = 112


def split_parts(values):
    upper = values.astype(BF16)
    lower = (values - upper.astype(F32)).astype(BF16)
    return (upper, lower)


def dot(a, b, ca=1, cb=0):
    return lax.dot_general(a, b, (((ca,), (cb,)), ((), ())), preferred_element_type=F32)


def iota(shape, axis):
    return lax.broadcasted_iota(jnp.int32, shape, axis)


def kernel(
    cls_dev, scale,
    pos_ref, teacher, student, head, freqs,
    grad_out, loss_out,
    out_z, in_z, out_x, in_x, t_all, w_all, h_all, f_out, f_in, f_rows,
    zs_ref, zt_ref, sin_ref, cos_ref, du_ref, dl_ref, gz_ref, gz_all,
    hg_ref, hx_out, hx_in, hz_out, hz_in, cl_all, send_sem, recv_sem,
):
    dp = lax.axis_index("dp")
    feat = lax.axis_index("feat")
    nz = lax.axis_size("dp") // NX
    ny = lax.axis_size("feat") // NC
    z, x = dp // NX, dp % NX
    y, c = feat // NC, feat % NC
    images, d_t = teacher.shape
    d_s = student.shape[1]
    half = freqs.shape[1]
    cap = 2 * images // (nz * NX)
    slots = nz * NX * cap
    part = d_t // (ny * NC)
    xrow = slots // NX

    def at_z(o):
        return {"dp": ((z + o) % nz) * NX + x, "feat": feat}

    def at_x(o):
        return {"dp": z * NX + (x + o) % NX, "feat": feat}

    def feat_of(dy, dc):
        return ((y + dy) % ny) * NC + (c + dc) % NC

    def at_f(dy, dc):
        return {"dp": dp, "feat": feat_of(dy, dc)}

    feat_peers = [(dy, dc) for dy in range(ny) for dc in range(NC) if (dy, dc) != (0, 0)]
    z_order = sorted(range(1, nz), key=lambda o: -min(o, nz - o))

    barrier = pltpu.get_barrier_semaphore()
    peers = [at_z(o) for o in z_order] + [at_x(o) for o in range(1, NX)] + [at_f(*p) for p in feat_peers]
    for peer in peers:
        pl.semaphore_signal(barrier, inc=1, device_id=peer, device_id_type=pl.DeviceIdType.MESH)

    started = []

    def send(src, dst, peer):
        k = len(started)
        copy = pltpu.make_async_remote_copy(
            src_ref=src,
            dst_ref=dst,
            send_sem=send_sem.at[k],
            recv_sem=recv_sem.at[k],
            device_id=peer,
            device_id_type=pl.DeviceIdType.MESH,
        )
        copy.start()
        started.append(copy)
        return copy

    def gather_start(src, dst):
        g = {}
        for h in (0, 1):
            g["up", h] = send(src(h), dst(feat, h), at_f(1, 0))
            g["down", 1 - h] = send(src(1 - h), dst(feat, 1 - h), at_f(ny - 1, 0))
        for h in (0, 1):
            g["own", h] = send(src(h), dst(feat, h), at_f(0, 1))
        return g

    def gather_relay(g, dst):
        below, above, far = feat_of(ny - 1, 0), feat_of(1, 0), feat_of(2, 0)
        for h in (0, 1):
            g["up", h].wait_recv()
            if h == 0:
                g["far", 0] = send(dst(below, 0), dst(below, 0), at_f(1, 0))
            g["pup", h] = send(dst(below, h), dst(below, h), at_f(0, 1))
            g["down", 1 - h].wait_recv()
            if h == 0:
                g["far", 1] = send(dst(above, 1), dst(above, 1), at_f(ny - 1, 0))
            g["pdown", 1 - h] = send(dst(above, 1 - h), dst(above, 1 - h), at_f(0, 1))
        for h in (0, 1):
            g["far", h].wait_recv()
            g["pfar", h] = send(dst(far, h), dst(far, h), at_f(0, 1))

    def gather_finish(g):
        for h in (0, 1):
            for name in ("own", "pup", "pdown", "pfar"):
                g[name, h].wait_recv()

    pos_row = jnp.broadcast_to(pos_ref[...].astype(F32), (images, images))
    pos_col = pos_row.T
    own_row = jnp.floor((pos_row + 0.5) * (1.0 / cls_dev))
    own_col = jnp.floor((pos_col + 0.5) * (1.0 / cls_dev))
    ahead = (own_row == own_col) & (iota((images, images), 0) < iota((images, images), 1))
    rank = jnp.sum(jnp.where(ahead, 1.0, 0.0), axis=0, keepdims=True)
    slot = own_row[:1] * cap + rank
    select = (iota((slots, images), 0).astype(F32) == slot).astype(F32).astype(BF16)
    tag = pos_col - own_col * cls_dev + 1.0
    tag_hi = jnp.floor(tag * (1.0 / 32.0))
    lane = iota((images, part), 1)
    tags = jnp.where(lane == 0, tag_hi, jnp.where(lane == 1, tag - 32.0 * tag_hi, 0.0)).astype(BF16)
    full_parts = d_s // part
    s_at = pl.multiple_of(jnp.minimum(feat, full_parts - 1) * part, part)
    wide = student[:, pl.ds(s_at, part)]
    is_tag = (jnp.zeros((images, part), jnp.int32) + feat) >= full_parts
    wide = jnp.where(is_tag, tags, wide)
    f_at = pl.multiple_of(feat * part, part)
    rows = jnp.concatenate([teacher[:, pl.ds(f_at, part)], wide], axis=1)
    out_z[...] = dot(select, rows).astype(BF16).reshape(out_z.shape)

    pl.semaphore_wait(barrier, len(peers))

    z_copies = [send(out_z.at[(z + o) % nz], in_z.at[o], at_z(o)) for o in z_order]
    in_z[0] = out_z[z]

    h_half = d_s // 2

    def h_src(h):
        return head.at[pl.ds(h * h_half, h_half), :]

    def h_dst(f, h):
        return h_all.at[pl.ds(h * h_half, h_half), pl.ds(pl.multiple_of(f * part, part), part)]

    h_gather = gather_start(h_src, h_dst)
    h_all[:, pl.ds(f_at, part)] = head[...]

    n_feat = ny * NC
    q = iota((part, part), 0)
    e2 = d_t // (nz * NX * n_feat)
    group = part // n_feat
    src_row = (q % group) // e2 * (n_feat * e2) + (q // group) * e2 + q % e2
    perm = (src_row == iota((part, part), 1)).astype(F32).astype(BF16)
    for b in range(d_t // part):
        moved = dot(perm, freqs[b * part : (b + 1) * part, :]).astype(BF16)
        f_out[:, b * group : (b + 1) * group, :] = moved.reshape(n_feat, group, half)
    def f_dst(f):
        return f_in.at[:, pl.ds(pl.multiple_of(f * half, half), half)]

    f_copies = [send(f_out.at[feat_of(*p)], f_dst(feat), at_f(*p)) for p in feat_peers]
    f_in[:, pl.ds(pl.multiple_of(feat * half, half), half)] = f_out[feat]

    for copy in z_copies:
        copy.wait_recv()
    q = iota((slots, slots), 0)
    src_row = (q % xrow) // cap * (NX * cap) + (q // xrow) * cap + q % cap
    perm = (src_row == iota((slots, slots), 1)).astype(F32).astype(BF16)
    out_x[...] = dot(perm, in_z[...].reshape(slots, 2 * part)).astype(BF16).reshape(out_x.shape)
    x_copies = [
        send(out_x.at[(x + o) % NX], in_x.at[pl.ds(o * xrow, xrow), :], at_x(o)) for o in (2, 1, 3)
    ]
    in_x[0:xrow, :] = out_x[x]
    gather_relay(h_gather, h_dst)
    for copy in x_copies:
        copy.wait_recv()

    s_half = slots // 2

    def x_src(which):
        return lambda h: in_x.at[pl.ds(h * s_half, s_half), pl.ds(which * part, part)]

    def x_dst(ref):
        return lambda f, h: ref.at[
            pl.ds(h * s_half, s_half), pl.ds(pl.multiple_of(f * part, part), part)
        ]

    w_gather = gather_start(x_src(1), x_dst(w_all))
    t_gather = gather_start(x_src(0), x_dst(t_all))
    t_all[:, pl.ds(f_at, part)] = in_x[:, :part]
    w_all[:, pl.ds(f_at, part)] = in_x[:, part:]
    gather_finish(h_gather)

    for copy in f_copies:
        copy.wait_recv()
    q = iota((part, part), 0)
    src_row = (q % (nz * e2)) // e2 * (NX * e2) + (q // (nz * e2)) * e2 + q % e2
    perm = (src_row == iota((part, part), 1)).astype(F32).astype(BF16)
    f_rows[...] = dot(perm, f_in[...]).astype(BF16)

    gather_relay(w_gather, x_dst(w_all))
    gather_relay(t_gather, x_dst(t_all))
    gather_finish(w_gather)

    for n in range(d_t // half):
        cols = slice(n * half, (n + 1) * half)
        projected = dot(w_all[:, :d_s], h_all[:, cols]).astype(BF16)
        product = dot(projected, freqs[cols, :])
        if n == 0:
            zs_ref[...] = product
        else:
            zs_ref[...] += product
    gather_finish(t_gather)
    zt_ref[...] = dot(t_all[...], freqs[...])

    block = 32

    def trig(i, _):
        r = pl.ds(pl.multiple_of(i * block, block), block)
        zs, zt = zs_ref[r, :], zt_ref[r, :]
        sin_s, cos_s = jnp.sin(zs), jnp.cos(zs)
        sin_ref[r, :] = sin_s
        cos_ref[r, :] = cos_s
        upper, lower = split_parts(cos_s - jnp.cos(zt))
        du_ref[r, :half] = upper
        dl_ref[r, :half] = lower
        upper, lower = split_parts(sin_s - jnp.sin(zt))
        du_ref[r, half:] = upper
        dl_ref[r, half:] = lower
        return 0

    lax.fori_loop(0, slots // block, trig, 0)

    tag_block = w_all[:, d_s : d_s + part]
    weight = jnp.where(iota((16, part), 1) == 0, 32.0, jnp.where(iota((16, part), 1) == 1, 1.0, 0.0))
    tag_row = dot(weight.astype(BF16), tag_block, 1, 1)[:1]
    tag_col = tag_block[:, 0:1].astype(F32) * 32.0 + tag_block[:, 1:2].astype(F32)
    alike = jnp.where((tag_row == tag_col) & (tag_col > 0.5), 1.0, 0.0)
    count = jnp.maximum(jnp.sum(alike, axis=1, keepdims=True), 1.0)
    member = alike.astype(BF16)
    sums_cos = dot(member, du_ref[:, :half]) + dot(member, dl_ref[:, :half])
    sums_sin = dot(member, du_ref[:, half:]) + dot(member, dl_ref[:, half:])
    grad_z = (-sin_ref[...] * sums_cos + cos_ref[...] * sums_sin) / count
    gz_ref[...] = grad_z.astype(BF16)

    def g_src(h):
        return gz_ref.at[pl.ds(h * s_half, s_half), :]

    def g_dst(f, h):
        return gz_all.at[pl.ds(h * s_half, s_half), pl.ds(pl.multiple_of(f * half, half), half)]

    g_gather = gather_start(g_src, g_dst)
    gz_all[:, pl.ds(pl.multiple_of(feat * half, half), half)] = gz_ref[...]

    norm = jnp.sum(sums_cos * sums_cos + sums_sin * sums_sin, axis=1, keepdims=True) / count
    wide_cls = loss_out.shape[1]
    holds = (iota((slots, wide_cls), 1).astype(F32) + 1.0) == tag_col
    per_class = jnp.sum(jnp.where(holds, norm, 0.0), axis=0, keepdims=True)
    counts = jnp.maximum(jnp.sum(jnp.where(holds, 1.0, 0.0), axis=0, keepdims=True), 1.0)
    cl_all[feat] = per_class / counts * (1.0 / (2.0 * half * n_feat))
    c_copies = [send(cl_all.at[feat], cl_all.at[feat], at_f(*p)) for p in feat_peers]

    gather_relay(g_gather, g_dst)
    gather_finish(g_gather)

    grad_u = dot(gz_all[...], f_rows[...], 1, 1)
    u_upper, u_lower = split_parts(grad_u)
    student_in = w_all[:, :d_s]
    partial = dot(u_upper, student_in, 0, 0) + dot(u_lower, student_in, 0, 0)
    hg_ref[...] = partial.reshape(hg_ref.shape)
    hx_out[...] = partial.astype(BF16).reshape(hx_out.shape)
    x_copies = [send(hx_out.at[(x + o) % NX], hx_in.at[o], at_x(o)) for o in (2, 1, 3)]
    total = hg_ref[x]
    for copy in c_copies:
        copy.wait_recv()
    loss_out[...] = jnp.sum(cl_all[...], axis=0)
    for copy in x_copies:
        copy.wait_recv()
    for o in range(1, NX):
        total += hx_in[o].astype(F32)
    for j in range(nz):
        hz_out[j] = total[j * e2 : (j + 1) * e2, :]
    z_copies = [send(hz_out.at[(z + o) % nz], hz_in.at[o], at_z(o)) for o in z_order]
    hz_in[0] = hz_out[z]
    for copy in z_copies:
        copy.wait_recv()
    grad_out[...] = jnp.sum(hz_in[...], axis=0) * scale
    for copy in started:
        copy.wait_send()


def on_device(teacher, student, head, freqs, labels, class_slot):
    n_dp = lax.axis_size("dp")
    n_feat = lax.axis_size("feat")
    images, d_t = teacher.shape
    d_s = student.shape[1]
    half = freqs.shape[1]
    cls_dev = class_slot.shape[0] // n_dp
    nz = n_dp // NX
    cap = 2 * images // n_dp
    slots = n_dp * cap
    part = d_t // n_feat
    rows_dev = d_t // (n_dp * n_feat)
    wide_cls = -(-cls_dev // 128) * 128
    position = class_slot.at[labels].get(mode="promise_in_bounds").reshape(1, images)
    vmem = pl.BlockSpec(memory_space=pltpu.VMEM)
    scratch = [
        pltpu.VMEM((nz, NX * cap, 2 * part), BF16),
        pltpu.VMEM((nz, NX * cap, 2 * part), BF16),
        pltpu.VMEM((NX, slots // NX, 2 * part), BF16),
        pltpu.VMEM((slots, 2 * part), BF16),
        pltpu.VMEM((slots, d_t), BF16),
        pltpu.VMEM((slots, d_t), BF16),
        pltpu.VMEM((d_s, d_t), BF16),
        pltpu.VMEM((n_feat, part, half), BF16),
        pltpu.VMEM((part, half * n_feat), BF16),
        pltpu.VMEM((part, half * n_feat), BF16),
        pltpu.VMEM((slots, half), F32),
        pltpu.VMEM((slots, half), F32),
        pltpu.VMEM((slots, half), F32),
        pltpu.VMEM((slots, half), F32),
        pltpu.VMEM((slots, 2 * half), BF16),
        pltpu.VMEM((slots, 2 * half), BF16),
        pltpu.VMEM((slots, half), BF16),
        pltpu.VMEM((slots, half * n_feat), BF16),
        pltpu.VMEM((NX, part // NX, d_s), F32),
        pltpu.VMEM((NX, part // NX, d_s), BF16),
        pltpu.VMEM((NX, part // NX, d_s), BF16),
        pltpu.VMEM((nz, rows_dev, d_s), F32),
        pltpu.VMEM((nz, rows_dev, d_s), F32),
        pltpu.VMEM((n_feat, 1, wide_cls), F32),
        pltpu.SemaphoreType.DMA((COPIES,)),
        pltpu.SemaphoreType.DMA((COPIES,)),
    ]
    grad, loss = pl.pallas_call(
        functools.partial(kernel, cls_dev, 1.0 / math.sqrt(images * n_dp)),
        out_shape=(
            jax.ShapeDtypeStruct((rows_dev, d_s), F32),
            jax.ShapeDtypeStruct((1, wide_cls), F32),
        ),
        in_specs=[vmem] * 5,
        out_specs=(vmem, vmem),
        scratch_shapes=scratch,
        compiler_params=pltpu.CompilerParams(
            collective_id=0, has_side_effects=True, vmem_limit_bytes=48 * 1024 * 1024
        ),
    )(position, teacher, student, head, freqs)
    return (grad, loss[0, :cls_dev])


def solution(mesh):
    in_specs = (P("dp", None), P("dp", None), P(None, "feat"), P(None, "feat"), P("dp"), P())
    out_specs = (P(("dp", "feat"), None), P("dp"))
    return jax.shard_map(
        on_device, mesh=mesh, in_specs=in_specs, out_specs=out_specs, check_vma=False
    )
```

```python
import functools
import math

import jax
import jax.numpy as jnp
from jax import lax
from jax.experimental import pallas as pl
from jax.experimental.pallas import tpu as pltpu
from jax.sharding import PartitionSpec as P

F32, BF16 = jnp.float32, jnp.bfloat16
NX, NC = 4, 2
COPIES = 120


def split_parts(values):
    upper = values.astype(BF16)
    lower = (values - upper.astype(F32)).astype(BF16)
    return (upper, lower)


def dot(a, b, ca=1, cb=0):
    return lax.dot_general(a, b, (((ca,), (cb,)), ((), ())), preferred_element_type=F32)


def iota(shape, axis):
    return lax.broadcasted_iota(jnp.int32, shape, axis)


def kernel(
    cls_dev, scale,
    teacher_hbm, student_hbm, head_hbm, freqs_hbm, labels_hbm, slot_hbm,
    grad_out, loss_out,
    t_part, s_part, freqs, slot_table, labels,
    out_w, out_t, in_w, in_t, xo_w, xo_t, xi_w, xi_t, t_all, w_all, h_all, f_mid, f_rows,
    zs_ref, zt_ref, sin_ref, cos_ref, du_ref, dl_ref, u_out, u_in, u_own, v_out, v_in,
    hg_ref, hx_out, hx_in, hz_out, hz_in, cl_all, send_sem, recv_sem, load_sem,
):
    dp = lax.axis_index("dp")
    feat = lax.axis_index("feat")
    nz = lax.axis_size("dp") // NX
    ny = lax.axis_size("feat") // NC
    z, x = dp // NX, dp % NX
    y, c = feat // NC, feat % NC
    images, d_t = teacher_hbm.shape
    d_s = student_hbm.shape[1]
    half = freqs_hbm.shape[1]
    cap = 2 * images // (nz * NX)
    slots = nz * NX * cap
    part = d_t // (ny * NC)
    xrow = slots // NX

    def at_z(o):
        return {"dp": ((z + o) % nz) * NX + x, "feat": feat}

    def at_x(o):
        return {"dp": z * NX + (x + o) % NX, "feat": feat}

    def feat_of(dy, dc):
        return ((y + dy) % ny) * NC + (c + dc) % NC

    def at_f(dy, dc):
        return {"dp": dp, "feat": feat_of(dy, dc)}

    feat_peers = [(dy, dc) for dy in range(ny) for dc in range(NC) if (dy, dc) != (0, 0)]
    z_order = sorted(range(1, nz), key=lambda o: -min(o, nz - o))

    barrier = pltpu.get_barrier_semaphore()
    peers = [at_z(o) for o in z_order] + [at_x(o) for o in range(1, NX)] + [at_f(*p) for p in feat_peers]
    for peer in peers:
        pl.semaphore_signal(barrier, inc=1, device_id=peer, device_id_type=pl.DeviceIdType.MESH)

    f_at = pl.multiple_of(feat * part, part)
    full_parts = d_s // part
    s_at = pl.multiple_of(jnp.minimum(feat, full_parts - 1) * part, part)
    loads = [
        pltpu.make_async_copy(src, dst, load_sem.at[k])
        for k, (src, dst) in enumerate(
            [
                (slot_hbm, slot_table),
                (teacher_hbm.at[:, pl.ds(f_at, part)], t_part),
                (student_hbm.at[:, pl.ds(s_at, part)], s_part),
                (freqs_hbm, freqs),
                (head_hbm, h_all.at[:, pl.ds(f_at, part)]),
                (labels_hbm, labels),
            ]
        )
    ]
    for load in loads:
        load.start()

    started = []

    def send(src, dst, peer):
        k = len(started)
        copy = pltpu.make_async_remote_copy(
            src_ref=src,
            dst_ref=dst,
            send_sem=send_sem.at[k],
            recv_sem=recv_sem.at[k],
            device_id=peer,
            device_id_type=pl.DeviceIdType.MESH,
        )
        copy.start()
        started.append(copy)
        return copy

    def gather_start(src, dst):
        g = {}
        for h in (0, 1):
            g["up", h] = send(src(h), dst(feat, h), at_f(1, 0))
            g["down", 1 - h] = send(src(1 - h), dst(feat, 1 - h), at_f(ny - 1, 0))
        for h in (0, 1):
            g["own", h] = send(src(h), dst(feat, h), at_f(0, 1))
        return g

    def gather_near(g, dst):
        below, above = feat_of(ny - 1, 0), feat_of(1, 0)
        for h in (0, 1):
            g["up", h].wait_recv()
            if h == 0:
                g["far", 0] = send(dst(below, 0), dst(below, 0), at_f(1, 0))
            g["pup", h] = send(dst(below, h), dst(below, h), at_f(0, 1))
            g["down", 1 - h].wait_recv()
            if h == 0:
                g["far", 1] = send(dst(above, 1), dst(above, 1), at_f(ny - 1, 0))
            g["pdown", 1 - h] = send(dst(above, 1 - h), dst(above, 1 - h), at_f(0, 1))

    def gather_far(g, dst):
        far = feat_of(2, 0)
        for h in (0, 1):
            g["far", h].wait_recv()
            g["pfar", h] = send(dst(far, h), dst(far, h), at_f(0, 1))

    def gather_finish(g):
        for h in (0, 1):
            for name in ("own", "pup", "pdown", "pfar"):
                g[name, h].wait_recv()

    loads[0].wait()
    loads[5].wait()
    lane = iota((8, images), 1)

    def look_up(i, found):
        for k in range(8):
            j = i * 8 + k
            found = jnp.where(lane == j, slot_table[labels[j]], found)
        return found

    found = lax.fori_loop(0, images // 8, look_up, jnp.zeros((8, images), jnp.int32))
    pos_row = jnp.broadcast_to(found[:1].astype(F32), (images, images))
    pos_col = pos_row.T
    own_row = jnp.floor((pos_row + 0.5) * (1.0 / cls_dev))
    own_col = jnp.floor((pos_col + 0.5) * (1.0 / cls_dev))
    ahead = (own_row == own_col) & (iota((images, images), 0) < iota((images, images), 1))
    rank = jnp.sum(jnp.where(ahead, 1.0, 0.0), axis=0, keepdims=True)
    slot = own_row[:1] * cap + rank
    select = (iota((slots, images), 0).astype(F32) == slot).astype(F32).astype(BF16)
    tag = pos_col - own_col * cls_dev + 1.0
    tag_hi = jnp.floor(tag * (1.0 / 32.0))
    lane = iota((images, part), 1)
    tags = jnp.where(lane == 0, tag_hi, jnp.where(lane == 1, tag - 32.0 * tag_hi, 0.0)).astype(BF16)
    loads[1].wait()
    loads[2].wait()
    is_tag = (jnp.zeros((images, part), jnp.int32) + feat) >= full_parts
    wide = jnp.where(is_tag, tags, s_part[...])
    out_w[...] = dot(select, wide).astype(BF16).reshape(out_w.shape)
    out_t[...] = dot(select, t_part[...]).astype(BF16).reshape(out_t.shape)

    loads[3].wait()
    n_feat = ny * NC
    q = iota((part, part), 0)
    k = iota((part, part), 1)
    e2 = d_t // (nz * NX * n_feat)
    group = part // n_feat
    by_feat = (q % group) // e2 * (n_feat * e2) + (q // group) * e2 + q % e2
    by_feat = (by_feat == k).astype(F32).astype(BF16)
    by_x = (q % (nz * e2)) // e2 * (NX * e2) + (q // (nz * e2)) * e2 + q % e2
    by_x = (by_x == k).astype(F32).astype(BF16)
    for b in range(d_t // part):
        moved = dot(by_feat, freqs[b * part : (b + 1) * part, :]).astype(BF16)
        f_mid[:, b * group : (b + 1) * group, :] = moved.reshape(n_feat, group, half)
    for f in range(n_feat):
        f_rows[f] = dot(by_x, f_mid[f]).astype(BF16)
    q = iota((slots, slots), 0)
    src_row = (q % xrow) // cap * (NX * cap) + (q // xrow) * cap + q % cap
    regroup = (src_row == iota((slots, slots), 1)).astype(F32).astype(BF16)

    pl.semaphore_wait(barrier, len(peers))

    z_copies = {}
    for name, out, into in (("w", out_w, in_w), ("t", out_t, in_t)):
        z_copies[name] = [send(out.at[(z + o) % nz], into.at[o], at_z(o)) for o in z_order]
        into[0] = out[z]

    h_half = d_s // 2

    def h_src(h):
        return head_hbm.at[pl.ds(h * h_half, h_half), :]

    def h_dst(f, h):
        return h_all.at[pl.ds(h * h_half, h_half), pl.ds(pl.multiple_of(f * part, part), part)]

    h_gather = gather_start(h_src, h_dst)
    gather_near(h_gather, h_dst)

    x_copies = {}
    for name, into, out, got in (("w", in_w, xo_w, xi_w), ("t", in_t, xo_t, xi_t)):
        for copy in z_copies[name]:
            copy.wait_recv()
        moved = dot(regroup, into[...].reshape(slots, part))
        out[...] = moved.astype(BF16).reshape(out.shape)
        x_copies[name] = [
            send(out.at[(x + o) % NX], got.at[pl.ds(o * xrow, xrow), :], at_x(o)) for o in (2, 1, 3)
        ]
        got[0:xrow, :] = out[x]
    gather_far(h_gather, h_dst)
    s_half = slots // 2

    def x_src(ref):
        return lambda h: ref.at[pl.ds(h * s_half, s_half), :]

    def x_dst(ref):
        return lambda f, h: ref.at[
            pl.ds(h * s_half, s_half), pl.ds(pl.multiple_of(f * part, part), part)
        ]

    gathers = {}
    for name, got, ref in (("w", xi_w, w_all), ("t", xi_t, t_all)):
        for copy in x_copies[name]:
            copy.wait_recv()
        gathers[name] = gather_start(x_src(got), x_dst(ref))
        ref[:, pl.ds(f_at, part)] = got[...]
    gather_near(gathers["w"], x_dst(w_all))
    gather_near(gathers["t"], x_dst(t_all))
    gather_far(gathers["w"], x_dst(w_all))
    gather_far(gathers["t"], x_dst(t_all))
    gather_finish(h_gather)
    loads[4].wait()
    gather_finish(gathers["w"])

    for n in range(d_t // half):
        cols = slice(n * half, (n + 1) * half)
        projected = dot(w_all[:, :d_s], h_all[:, cols]).astype(BF16)
        product = dot(projected, freqs[cols, :])
        if n == 0:
            zs_ref[...] = product
        else:
            zs_ref[...] += product
    gather_finish(gathers["t"])
    zt_ref[...] = dot(t_all[...], freqs[...])

    block = 32

    def trig(i, _):
        r = pl.ds(pl.multiple_of(i * block, block), block)
        zs, zt = zs_ref[r, :], zt_ref[r, :]
        sin_s, cos_s = jnp.sin(zs), jnp.cos(zs)
        sin_ref[r, :] = sin_s
        cos_ref[r, :] = cos_s
        upper, lower = split_parts(cos_s - jnp.cos(zt))
        du_ref[r, :half] = upper
        dl_ref[r, :half] = lower
        upper, lower = split_parts(sin_s - jnp.sin(zt))
        du_ref[r, half:] = upper
        dl_ref[r, half:] = lower
        return 0

    lax.fori_loop(0, slots // block, trig, 0)

    tag_block = w_all[:, d_s : d_s + part]
    weight = jnp.where(iota((16, part), 1) == 0, 32.0, jnp.where(iota((16, part), 1) == 1, 1.0, 0.0))
    tag_row = dot(weight.astype(BF16), tag_block, 1, 1)[:1]
    tag_col = tag_block[:, 0:1].astype(F32) * 32.0 + tag_block[:, 1:2].astype(F32)
    alike = jnp.where((tag_row == tag_col) & (tag_col > 0.5), 1.0, 0.0)
    count = jnp.maximum(jnp.sum(alike, axis=1, keepdims=True), 1.0)
    member = alike.astype(BF16)
    sums_cos = dot(member, du_ref[:, :half]) + dot(member, dl_ref[:, :half])
    sums_sin = dot(member, du_ref[:, half:]) + dot(member, dl_ref[:, half:])
    grad_z = (-sin_ref[...] * sums_cos + cos_ref[...] * sums_sin) / count
    grad_z = grad_z.astype(BF16)

    y_order = (2, 1, 3, 0)
    u_copies = {}
    for dy in y_order:
        u_out[dy] = dot(grad_z, f_rows[feat_of(dy, 1)], 1, 1)
        u_copies[dy] = send(u_out.at[dy], u_in.at[dy], at_f(0, 1))
    for dy in y_order:
        u_own[dy] = dot(grad_z, f_rows[feat_of(dy, 0)], 1, 1)
    y_copies = {}
    for dy in y_order[:-1]:
        u_copies[dy].wait_recv()
        v_out[dy] = (u_own[dy] + u_in[dy]).astype(BF16)
        y_copies[dy] = send(v_out.at[dy], v_in.at[dy], at_f(dy, 0))

    norm = jnp.sum(sums_cos * sums_cos + sums_sin * sums_sin, axis=1, keepdims=True) / count
    wide_cls = loss_out.shape[1]
    holds = (iota((slots, wide_cls), 1).astype(F32) + 1.0) == tag_col
    per_class = jnp.sum(jnp.where(holds, norm, 0.0), axis=0, keepdims=True)
    counts = jnp.maximum(jnp.sum(jnp.where(holds, 1.0, 0.0), axis=0, keepdims=True), 1.0)
    cl_all[feat] = per_class / counts * (1.0 / (2.0 * half * n_feat))
    c_copies = [send(cl_all.at[feat], cl_all.at[feat], at_f(*p)) for p in feat_peers]

    u_copies[0].wait_recv()
    grad_u = u_own[0] + u_in[0]
    for dy in y_order[:-1]:
        y_copies[dy].wait_recv()
        grad_u += v_in[dy].astype(F32)
    u_upper, u_lower = split_parts(grad_u)
    student_in = w_all[:, :d_s]
    partial = dot(u_upper, student_in, 0, 0) + dot(u_lower, student_in, 0, 0)
    hg_ref[...] = partial.reshape(hg_ref.shape)
    hx_out[...] = partial.astype(BF16).reshape(hx_out.shape)
    x_copies = [send(hx_out.at[(x + o) % NX], hx_in.at[o], at_x(o)) for o in (2, 1, 3)]
    total = hg_ref[x]
    for copy in c_copies:
        copy.wait_recv()
    loss_out[...] = jnp.sum(cl_all[...], axis=0)
    for copy in x_copies:
        copy.wait_recv()
    for o in range(1, NX):
        total += hx_in[o].astype(F32)
    for j in range(nz):
        hz_out[j] = total[j * e2 : (j + 1) * e2, :]
    z_copies = [send(hz_out.at[(z + o) % nz], hz_in.at[o], at_z(o)) for o in z_order]
    hz_in[0] = hz_out[z]
    for copy in z_copies:
        copy.wait_recv()
    grad_out[...] = jnp.sum(hz_in[...], axis=0) * scale
    for copy in started:
        copy.wait_send()


def on_device(teacher, student, head, freqs, labels, class_slot):
    n_dp = lax.axis_size("dp")
    n_feat = lax.axis_size("feat")
    images, d_t = teacher.shape
    d_s = student.shape[1]
    half = freqs.shape[1]
    cls_dev = class_slot.shape[0] // n_dp
    nz = n_dp // NX
    cap = 2 * images // n_dp
    slots = n_dp * cap
    part = d_t // n_feat
    rows_dev = d_t // (n_dp * n_feat)
    wide_cls = -(-cls_dev // 128) * 128
    vmem = pl.BlockSpec(memory_space=pltpu.VMEM)
    hbm = pl.BlockSpec(memory_space=pltpu.HBM)
    scratch = [
        pltpu.VMEM((images, part), BF16),
        pltpu.VMEM((images, part), BF16),
        pltpu.VMEM((d_t, half), BF16),
        pltpu.SMEM(class_slot.shape, jnp.int32),
        pltpu.SMEM(labels.shape, jnp.int32),
        pltpu.VMEM((nz, NX * cap, part), BF16),
        pltpu.VMEM((nz, NX * cap, part), BF16),
        pltpu.VMEM((nz, NX * cap, part), BF16),
        pltpu.VMEM((nz, NX * cap, part), BF16),
        pltpu.VMEM((NX, slots // NX, part), BF16),
        pltpu.VMEM((NX, slots // NX, part), BF16),
        pltpu.VMEM((slots, part), BF16),
        pltpu.VMEM((slots, part), BF16),
        pltpu.VMEM((slots, d_t), BF16),
        pltpu.VMEM((slots, d_t), BF16),
        pltpu.VMEM((d_s, d_t), BF16),
        pltpu.VMEM((n_feat, part, half), BF16),
        pltpu.VMEM((n_feat, part, half), BF16),
        pltpu.VMEM((slots, half), F32),
        pltpu.VMEM((slots, half), F32),
        pltpu.VMEM((slots, half), F32),
        pltpu.VMEM((slots, half), F32),
        pltpu.VMEM((slots, 2 * half), BF16),
        pltpu.VMEM((slots, 2 * half), BF16),
        pltpu.VMEM((n_feat // NC, slots, part), F32),
        pltpu.VMEM((n_feat // NC, slots, part), F32),
        pltpu.VMEM((n_feat // NC, slots, part), F32),
        pltpu.VMEM((n_feat // NC, slots, part), BF16),
        pltpu.VMEM((n_feat // NC, slots, part), BF16),
        pltpu.VMEM((NX, part // NX, d_s), F32),
        pltpu.VMEM((NX, part // NX, d_s), BF16),
        pltpu.VMEM((NX, part // NX, d_s), BF16),
        pltpu.VMEM((nz, rows_dev, d_s), F32),
        pltpu.VMEM((nz, rows_dev, d_s), F32),
        pltpu.VMEM((n_feat, 1, wide_cls), F32),
        pltpu.SemaphoreType.DMA((COPIES,)),
        pltpu.SemaphoreType.DMA((COPIES,)),
        pltpu.SemaphoreType.DMA((6,)),
    ]
    grad, loss = pl.pallas_call(
        functools.partial(kernel, cls_dev, 1.0 / math.sqrt(images * n_dp)),
        out_shape=(
            jax.ShapeDtypeStruct((rows_dev, d_s), F32),
            jax.ShapeDtypeStruct((1, wide_cls), F32),
        ),
        in_specs=[hbm] * 6,
        out_specs=(vmem, vmem),
        scratch_shapes=scratch,
        compiler_params=pltpu.CompilerParams(
            collective_id=0, has_side_effects=True, vmem_limit_bytes=66_900_000
        ),
    )(teacher, student, head, freqs, labels, class_slot)
    return (grad, loss[0, :cls_dev])


def solution(mesh):
    in_specs = (P("dp", None), P("dp", None), P(None, "feat"), P(None, "feat"), P("dp"), P())
    out_specs = (P(("dp", "feat"), None), P("dp"))
    return jax.shard_map(
        on_device, mesh=mesh, in_specs=in_specs, out_specs=out_specs, check_vma=False
    )
```

```python
import functools
import math

import jax
import jax.numpy as jnp
from jax import lax
from jax.experimental import pallas as pl
from jax.experimental.pallas import tpu as pltpu
from jax.sharding import PartitionSpec as P

F32, BF16 = jnp.float32, jnp.bfloat16
NX, NC = 4, 2
COPIES = 120


def split_parts(values):
    upper = values.astype(BF16)
    lower = (values - upper.astype(F32)).astype(BF16)
    return (upper, lower)


def dot(a, b, ca=1, cb=0):
    return lax.dot_general(a, b, (((ca,), (cb,)), ((), ())), preferred_element_type=F32)


def iota(shape, axis):
    return lax.broadcasted_iota(jnp.int32, shape, axis)


def kernel(
    cls_dev, scale,
    teacher_hbm, student_hbm, head_hbm, freqs_hbm, labels_hbm, slot_hbm,
    grad_out, loss_out,
    t_part, s_part, freqs, slot_table, labels,
    out_w, out_t, in_w, in_t, xo_w, xo_t, t_all, w_all, h_all, f_mid, f_rows,
    zs_ref, zt_ref, cost_ref, sint_ref, sin_ref, cos_ref, du_ref, dl_ref, u_out, u_in, u_own, v_out, v_in,
    hg_ref, hx_out, hx_in, hz_out, hz_in, cl_out, cl_in, send_sem, recv_sem, load_sem,
):
    dp = lax.axis_index("dp")
    feat = lax.axis_index("feat")
    nz = lax.axis_size("dp") // NX
    ny = lax.axis_size("feat") // NC
    z, x = dp // NX, dp % NX
    y, c = feat // NC, feat % NC
    images, d_t = teacher_hbm.shape
    d_s = student_hbm.shape[1]
    half = freqs_hbm.shape[1]
    cap = 2 * images // (nz * NX)
    slots = nz * NX * cap
    part = d_t // (ny * NC)
    xrow = slots // NX

    def at_z(o):
        return {"dp": ((z + o) % nz) * NX + x, "feat": feat}

    def at_x(o):
        return {"dp": z * NX + (x + o) % NX, "feat": feat}

    def feat_of(dy, dc):
        return ((y + dy) % ny) * NC + (c + dc) % NC

    def at_f(dy, dc):
        return {"dp": dp, "feat": feat_of(dy, dc)}

    def at_xy(ox, dy):
        return {"dp": z * NX + (x + ox) % NX, "feat": feat_of(dy, 0)}

    def hops(o, n):
        return min(o, n - o)

    plane = [(ox, dy) for ox in range(NX) for dy in range(ny) if (ox, dy) != (0, 0)]
    plane.sort(key=lambda p: -hops(p[0], NX) - hops(p[1], ny))
    z_order = sorted(range(1, nz), key=lambda o: -min(o, nz - o))

    barrier = pltpu.get_barrier_semaphore()
    peers = [at_z(o) for o in z_order] + [at_xy(*p) for p in plane] + [at_f(0, 1)]
    for peer in peers:
        pl.semaphore_signal(barrier, inc=1, device_id=peer, device_id_type=pl.DeviceIdType.MESH)

    f_at = pl.multiple_of(feat * part, part)
    full_parts = d_s // part
    s_at = pl.multiple_of(jnp.minimum(feat, full_parts - 1) * part, part)
    loads = [
        pltpu.make_async_copy(src, dst, load_sem.at[k])
        for k, (src, dst) in enumerate(
            [
                (slot_hbm, slot_table),
                (teacher_hbm.at[:, pl.ds(f_at, part)], t_part),
                (student_hbm.at[:, pl.ds(s_at, part)], s_part),
                (freqs_hbm, freqs),
                (head_hbm, h_all.at[:, pl.ds(f_at, part)]),
                (labels_hbm, labels),
            ]
        )
    ]
    for load in loads:
        load.start()

    started = []

    def send(src, dst, peer):
        k = len(started)
        copy = pltpu.make_async_remote_copy(
            src_ref=src,
            dst_ref=dst,
            send_sem=send_sem.at[k],
            recv_sem=recv_sem.at[k],
            device_id=peer,
            device_id_type=pl.DeviceIdType.MESH,
        )
        copy.start()
        started.append(copy)
        return copy

    def gather_start(src, dst):
        g = {}
        for h in (0, 1):
            g["up", h] = send(src(h), dst(feat, h), at_f(1, 0))
            g["down", 1 - h] = send(src(1 - h), dst(feat, 1 - h), at_f(ny - 1, 0))
        for h in (0, 1):
            g["own", h] = send(src(h), dst(feat, h), at_f(0, 1))
        return g

    def gather_near(g, dst):
        below, above = feat_of(ny - 1, 0), feat_of(1, 0)
        for h in (0, 1):
            g["up", h].wait_recv()
            if h == 0:
                g["far", 0] = send(dst(below, 0), dst(below, 0), at_f(1, 0))
            g["pup", h] = send(dst(below, h), dst(below, h), at_f(0, 1))
            g["down", 1 - h].wait_recv()
            if h == 0:
                g["far", 1] = send(dst(above, 1), dst(above, 1), at_f(ny - 1, 0))
            g["pdown", 1 - h] = send(dst(above, 1 - h), dst(above, 1 - h), at_f(0, 1))

    def gather_far(g, dst):
        far = feat_of(2, 0)
        for h in (0, 1):
            g["far", h].wait_recv()
            g["pfar", h] = send(dst(far, h), dst(far, h), at_f(0, 1))

    def gather_finish(g):
        for h in (0, 1):
            for name in ("own", "pup", "pdown", "pfar"):
                g[name, h].wait_recv()

    loads[0].wait()
    loads[5].wait()
    lane = iota((8, images), 1)

    def look_up(i, found):
        for k in range(8):
            j = i * 8 + k
            found = jnp.where(lane == j, slot_table[labels[j]], found)
        return found

    found = lax.fori_loop(0, images // 8, look_up, jnp.zeros((8, images), jnp.int32))
    pos_row = jnp.broadcast_to(found[:1].astype(F32), (images, images))
    pos_col = pos_row.T
    own_row = jnp.floor((pos_row + 0.5) * (1.0 / cls_dev))
    own_col = jnp.floor((pos_col + 0.5) * (1.0 / cls_dev))
    ahead = (own_row == own_col) & (iota((images, images), 0) < iota((images, images), 1))
    rank = jnp.sum(jnp.where(ahead, 1.0, 0.0), axis=0, keepdims=True)
    slot = own_row[:1] * cap + rank
    select = (iota((slots, images), 0).astype(F32) == slot).astype(F32).astype(BF16)
    tag = pos_col - own_col * cls_dev + 1.0
    tag_hi = jnp.floor(tag * (1.0 / 32.0))
    lane = iota((images, part), 1)
    tags = jnp.where(lane == 0, tag_hi, jnp.where(lane == 1, tag - 32.0 * tag_hi, 0.0)).astype(BF16)
    loads[1].wait()
    loads[2].wait()
    is_tag = (jnp.zeros((images, part), jnp.int32) + feat) >= full_parts
    wide = jnp.where(is_tag, tags, s_part[...])
    out_w[...] = dot(select, wide).astype(BF16).reshape(out_w.shape)
    out_t[...] = dot(select, t_part[...]).astype(BF16).reshape(out_t.shape)

    pl.semaphore_wait(barrier, len(peers))

    z_copies = {}
    for name, out, into in (("t", out_t, in_t), ("w", out_w, in_w)):
        z_copies[name] = [send(out.at[(z + o) % nz], into.at[o], at_z(o)) for o in z_order]
        into[0] = out[z]

    h_half = d_s // 2

    def h_src(h):
        return head_hbm.at[pl.ds(h * h_half, h_half), :]

    def h_dst(f, h):
        return h_all.at[pl.ds(h * h_half, h_half), pl.ds(pl.multiple_of(f * part, part), part)]

    h_gather = gather_start(h_src, h_dst)
    loads[3].wait()
    n_feat = ny * NC
    q = iota((part, part), 0)
    k = iota((part, part), 1)
    e2 = d_t // (nz * NX * n_feat)
    group = part // n_feat
    by_feat = (q % group) // e2 * (n_feat * e2) + (q // group) * e2 + q % e2
    by_feat = (by_feat == k).astype(F32).astype(BF16)
    by_x = (q % (nz * e2)) // e2 * (NX * e2) + (q // (nz * e2)) * e2 + q % e2
    by_x = (by_x == k).astype(F32).astype(BF16)
    for b in range(d_t // part):
        moved = dot(by_feat, freqs[b * part : (b + 1) * part, :]).astype(BF16)
        f_mid[:, b * group : (b + 1) * group, :] = moved.reshape(n_feat, group, half)
    for f in range(n_feat):
        f_rows[f] = dot(by_x, f_mid[f]).astype(BF16)
    q = iota((slots, slots), 0)
    src_row = (q % xrow) // cap * (NX * cap) + (q // xrow) * cap + q % cap
    regroup = (src_row == iota((slots, slots), 1)).astype(F32).astype(BF16)

    gather_near(h_gather, h_dst)

    chunks = {}
    for name, into, out, got in (("t", in_t, xo_t, t_all), ("w", in_w, xo_w, w_all)):
        for copy in z_copies[name]:
            copy.wait_recv()
        moved = dot(regroup, into[...].reshape(slots, part))
        out[...] = moved.astype(BF16).reshape(out.shape)
        chunks[name] = {
            (ox, dy): send(
                out.at[(x + ox) % NX], got.at[pl.ds(ox * xrow, xrow), pl.ds(f_at, part)], at_xy(ox, dy)
            )
            for ox, dy in plane
        }
        got[0:xrow, pl.ds(f_at, part)] = out[x]
    gather_far(h_gather, h_dst)
    forwards = {}
    for name, got in (("t", t_all), ("w", w_all)):
        forwards[name] = []
        for dy in (0, 1, 3, 2):
            for ox in range(NX):
                if (ox, dy) != (0, 0):
                    chunks[name][ox, dy].wait_recv()
            lanes = pl.ds(pl.multiple_of(feat_of(ny - dy, 0) * part, part), part)
            forwards[name].append(send(got.at[:, lanes], got.at[:, lanes], at_f(0, 1)))
    gather_finish(h_gather)
    loads[4].wait()
    for copy in forwards["t"]:
        copy.wait_recv()
    zt_ref[...] = dot(t_all[...], freqs[...])

    block = 32

    def trig_t(i, _):
        r = pl.ds(pl.multiple_of(i * block, block), block)
        zt = zt_ref[r, :]
        cost_ref[r, :] = jnp.cos(zt)
        sint_ref[r, :] = jnp.sin(zt)
        return 0

    lax.fori_loop(0, slots // block, trig_t, 0)
    for copy in forwards["w"]:
        copy.wait_recv()
    for n in range(d_t // half):
        cols = slice(n * half, (n + 1) * half)
        projected = dot(w_all[:, :d_s], h_all[:, cols]).astype(BF16)
        product = dot(projected, freqs[cols, :])
        if n == 0:
            zs_ref[...] = product
        else:
            zs_ref[...] += product

    def trig(i, _):
        r = pl.ds(pl.multiple_of(i * block, block), block)
        zs = zs_ref[r, :]
        sin_s, cos_s = jnp.sin(zs), jnp.cos(zs)
        sin_ref[r, :] = sin_s
        cos_ref[r, :] = cos_s
        upper, lower = split_parts(cos_s - cost_ref[r, :])
        du_ref[r, :half] = upper
        dl_ref[r, :half] = lower
        upper, lower = split_parts(sin_s - sint_ref[r, :])
        du_ref[r, half:] = upper
        dl_ref[r, half:] = lower
        return 0

    lax.fori_loop(0, slots // block, trig, 0)

    tag_block = w_all[:, d_s : d_s + part]
    weight = jnp.where(iota((16, part), 1) == 0, 32.0, jnp.where(iota((16, part), 1) == 1, 1.0, 0.0))
    tag_row = dot(weight.astype(BF16), tag_block, 1, 1)[:1]
    tag_col = tag_block[:, 0:1].astype(F32) * 32.0 + tag_block[:, 1:2].astype(F32)
    alike = jnp.where((tag_row == tag_col) & (tag_col > 0.5), 1.0, 0.0)
    count = jnp.maximum(jnp.sum(alike, axis=1, keepdims=True), 1.0)
    member = alike.astype(BF16)
    sums_cos = dot(member, du_ref[:, :half]) + dot(member, dl_ref[:, :half])
    sums_sin = dot(member, du_ref[:, half:]) + dot(member, dl_ref[:, half:])
    grad_z = (-sin_ref[...] * sums_cos + cos_ref[...] * sums_sin) / count
    grad_z = grad_z.astype(BF16)

    y_order = (2, 1, 3, 0)
    u_copies = {}
    for dy in y_order:
        u_out[dy] = dot(grad_z, f_rows[feat_of(dy, 1)], 1, 1)
        u_copies[dy] = send(u_out.at[dy], u_in.at[dy], at_f(0, 1))
    for dy in y_order:
        u_own[dy] = dot(grad_z, f_rows[feat_of(dy, 0)], 1, 1)
    y_copies = {}
    for dy in y_order[:-1]:
        u_copies[dy].wait_recv()
        v_out[dy] = (u_own[dy] + u_in[dy]).astype(BF16)
        y_copies[dy] = send(v_out.at[dy], v_in.at[dy], at_f(dy, 0))

    norm = jnp.sum(sums_cos * sums_cos + sums_sin * sums_sin, axis=1, keepdims=True) / count
    wide_cls = loss_out.shape[1]
    holds = (iota((slots, wide_cls), 1).astype(F32) + 1.0) == tag_col
    per_class = jnp.sum(jnp.where(holds, norm, 0.0), axis=0, keepdims=True)
    counts = jnp.maximum(jnp.sum(jnp.where(holds, 1.0, 0.0), axis=0, keepdims=True), 1.0)
    cl_out[0] = per_class / counts * (1.0 / (2.0 * half * n_feat))
    pair = send(cl_out.at[0], cl_in.at[0], at_f(0, 1))

    u_copies[0].wait_recv()
    grad_u = u_own[0] + u_in[0]
    for dy in y_order[:-1]:
        y_copies[dy].wait_recv()
        grad_u += v_in[dy].astype(F32)
    u_upper, u_lower = split_parts(grad_u)
    student_in = w_all[:, :d_s]
    partial = dot(u_upper, student_in, 0, 0) + dot(u_lower, student_in, 0, 0)
    hg_ref[...] = partial.reshape(hg_ref.shape)
    hx_out[...] = partial.astype(BF16).reshape(hx_out.shape)
    x_copies = [send(hx_out.at[(x + o) % NX], hx_in.at[o], at_x(o)) for o in (2, 1, 3)]
    total = hg_ref[x]
    pair.wait_recv()
    cl_out[1] = cl_out[0] + cl_in[0]
    c_copies = [send(cl_out.at[1], cl_in.at[dy], at_f(dy, 0)) for dy in range(1, ny)]
    for copy in x_copies:
        copy.wait_recv()
    for o in range(1, NX):
        total += hx_in[o].astype(F32)
    for j in range(nz):
        hz_out[j] = total[j * e2 : (j + 1) * e2, :]
    z_copies = [send(hz_out.at[(z + o) % nz], hz_in.at[o], at_z(o)) for o in z_order]
    hz_in[0] = hz_out[z]
    for copy in c_copies:
        copy.wait_recv()
    loss = cl_out[1]
    for dy in range(1, ny):
        loss += cl_in[dy]
    loss_out[...] = loss
    for copy in z_copies:
        copy.wait_recv()
    grad_out[...] = jnp.sum(hz_in[...], axis=0) * scale
    for copy in started:
        copy.wait_send()


def on_device(teacher, student, head, freqs, labels, class_slot):
    n_dp = lax.axis_size("dp")
    n_feat = lax.axis_size("feat")
    images, d_t = teacher.shape
    d_s = student.shape[1]
    half = freqs.shape[1]
    cls_dev = class_slot.shape[0] // n_dp
    nz = n_dp // NX
    cap = 2 * images // n_dp
    slots = n_dp * cap
    part = d_t // n_feat
    rows_dev = d_t // (n_dp * n_feat)
    wide_cls = -(-cls_dev // 128) * 128
    vmem = pl.BlockSpec(memory_space=pltpu.VMEM)
    hbm = pl.BlockSpec(memory_space=pltpu.HBM)
    scratch = [
        pltpu.VMEM((images, part), BF16),
        pltpu.VMEM((images, part), BF16),
        pltpu.VMEM((d_t, half), BF16),
        pltpu.SMEM(class_slot.shape, jnp.int32),
        pltpu.SMEM(labels.shape, jnp.int32),
        pltpu.VMEM((nz, NX * cap, part), BF16),
        pltpu.VMEM((nz, NX * cap, part), BF16),
        pltpu.VMEM((nz, NX * cap, part), BF16),
        pltpu.VMEM((nz, NX * cap, part), BF16),
        pltpu.VMEM((NX, slots // NX, part), BF16),
        pltpu.VMEM((NX, slots // NX, part), BF16),
        pltpu.VMEM((slots, d_t), BF16),
        pltpu.VMEM((slots, d_t), BF16),
        pltpu.VMEM((d_s, d_t), BF16),
        pltpu.VMEM((n_feat, part, half), BF16),
        pltpu.VMEM((n_feat, part, half), BF16),
        pltpu.VMEM((slots, half), F32),
        pltpu.VMEM((slots, half), F32),
        pltpu.VMEM((slots, half), F32),
        pltpu.VMEM((slots, half), F32),
        pltpu.VMEM((slots, half), F32),
        pltpu.VMEM((slots, half), F32),
        pltpu.VMEM((slots, 2 * half), BF16),
        pltpu.VMEM((slots, 2 * half), BF16),
        pltpu.VMEM((n_feat // NC, slots, part), F32),
        pltpu.VMEM((n_feat // NC, slots, part), F32),
        pltpu.VMEM((n_feat // NC, slots, part), F32),
        pltpu.VMEM((n_feat // NC, slots, part), BF16),
        pltpu.VMEM((n_feat // NC, slots, part), BF16),
        pltpu.VMEM((NX, part // NX, d_s), F32),
        pltpu.VMEM((NX, part // NX, d_s), BF16),
        pltpu.VMEM((NX, part // NX, d_s), BF16),
        pltpu.VMEM((nz, rows_dev, d_s), F32),
        pltpu.VMEM((nz, rows_dev, d_s), F32),
        pltpu.VMEM((2, 1, wide_cls), F32),
        pltpu.VMEM((n_feat // NC, 1, wide_cls), F32),
        pltpu.SemaphoreType.DMA((COPIES,)),
        pltpu.SemaphoreType.DMA((COPIES,)),
        pltpu.SemaphoreType.DMA((6,)),
    ]
    grad, loss = pl.pallas_call(
        functools.partial(kernel, cls_dev, 1.0 / math.sqrt(images * n_dp)),
        out_shape=(
            jax.ShapeDtypeStruct((rows_dev, d_s), F32),
            jax.ShapeDtypeStruct((1, wide_cls), F32),
        ),
        in_specs=[hbm] * 6,
        out_specs=(vmem, vmem),
        scratch_shapes=scratch,
        compiler_params=pltpu.CompilerParams(
            collective_id=0, has_side_effects=True, vmem_limit_bytes=66_900_000
        ),
    )(teacher, student, head, freqs, labels, class_slot)
    return (grad, loss[0, :cls_dev])


def solution(mesh):
    in_specs = (P("dp", None), P("dp", None), P(None, "feat"), P(None, "feat"), P("dp"), P())
    out_specs = (P(("dp", "feat"), None), P("dp"))
    return jax.shard_map(
        on_device, mesh=mesh, in_specs=in_specs, out_specs=out_specs, check_vma=False
    )
```

```python
import functools
import math

import jax
import jax.numpy as jnp
from jax import lax
from jax.experimental import pallas as pl
from jax.experimental.pallas import tpu as pltpu
from jax.sharding import PartitionSpec as P

F32, BF16 = jnp.float32, jnp.bfloat16
NX, NC = 4, 2
COPIES = 120


def split_parts(values):
    upper = values.astype(BF16)
    lower = (values - upper.astype(F32)).astype(BF16)
    return (upper, lower)


def dot(a, b, ca=1, cb=0):
    return lax.dot_general(a, b, (((ca,), (cb,)), ((), ())), preferred_element_type=F32)


def iota(shape, axis):
    return lax.broadcasted_iota(jnp.int32, shape, axis)


def kernel(
    cls_dev, scale,
    teacher_hbm, student_hbm, head_hbm, freqs_hbm, labels_hbm, slot_hbm,
    grad_out, loss_out,
    t_part, s_part, freqs, slot_table, labels,
    out_w, out_t, in_w, in_t, xo_w, xo_t, t_all, w_all, h_all, f_mid, f_rows, f_pair,
    zs_ref, zt_ref, cost_ref, sint_ref, sin_ref, cos_ref, du_ref, dl_ref, gz_out, gz_in, u_own, v_out, v_in,
    hg_ref, hx_out, hx_in, hz_out, hz_in, cl_out, cl_in, send_sem, recv_sem, load_sem,
):
    dp = lax.axis_index("dp")
    feat = lax.axis_index("feat")
    nz = lax.axis_size("dp") // NX
    ny = lax.axis_size("feat") // NC
    z, x = dp // NX, dp % NX
    y, c = feat // NC, feat % NC
    images, d_t = teacher_hbm.shape
    d_s = student_hbm.shape[1]
    half = freqs_hbm.shape[1]
    cap = 2 * images // (nz * NX)
    slots = nz * NX * cap
    part = d_t // (ny * NC)
    xrow = slots // NX

    def at_z(o):
        return {"dp": ((z + o) % nz) * NX + x, "feat": feat}

    def at_x(o):
        return {"dp": z * NX + (x + o) % NX, "feat": feat}

    def feat_of(dy, dc):
        return ((y + dy) % ny) * NC + (c + dc) % NC

    def at_f(dy, dc):
        return {"dp": dp, "feat": feat_of(dy, dc)}

    def at_xy(ox, dy):
        return {"dp": z * NX + (x + ox) % NX, "feat": feat_of(dy, 0)}

    def hops(o, n):
        return min(o, n - o)

    plane = [(ox, dy) for ox in range(NX) for dy in range(ny) if (ox, dy) != (0, 0)]
    plane.sort(key=lambda p: -hops(p[0], NX) - hops(p[1], ny))
    z_order = sorted(range(1, nz), key=lambda o: -min(o, nz - o))

    barrier = pltpu.get_barrier_semaphore()
    peers = [at_z(o) for o in z_order] + [at_xy(*p) for p in plane] + [at_f(0, 1)]
    for peer in peers:
        pl.semaphore_signal(barrier, inc=1, device_id=peer, device_id_type=pl.DeviceIdType.MESH)

    f_at = pl.multiple_of(feat * part, part)
    full_parts = d_s // part
    s_at = pl.multiple_of(jnp.minimum(feat, full_parts - 1) * part, part)
    loads = [
        pltpu.make_async_copy(src, dst, load_sem.at[k])
        for k, (src, dst) in enumerate(
            [
                (slot_hbm, slot_table),
                (teacher_hbm.at[:, pl.ds(f_at, part)], t_part),
                (student_hbm.at[:, pl.ds(s_at, part)], s_part),
                (freqs_hbm, freqs),
                (head_hbm, h_all.at[:, pl.ds(f_at, part)]),
                (labels_hbm, labels),
            ]
        )
    ]
    for load in loads:
        load.start()

    started = []

    def send(src, dst, peer):
        k = len(started)
        copy = pltpu.make_async_remote_copy(
            src_ref=src,
            dst_ref=dst,
            send_sem=send_sem.at[k],
            recv_sem=recv_sem.at[k],
            device_id=peer,
            device_id_type=pl.DeviceIdType.MESH,
        )
        copy.start()
        started.append(copy)
        return copy

    def gather_start(src, dst):
        g = {}
        for h in (0, 1):
            g["up", h] = send(src(h), dst(feat, h), at_f(1, 0))
            g["down", 1 - h] = send(src(1 - h), dst(feat, 1 - h), at_f(ny - 1, 0))
        for h in (0, 1):
            g["own", h] = send(src(h), dst(feat, h), at_f(0, 1))
        return g

    def gather_near(g, dst):
        below, above = feat_of(ny - 1, 0), feat_of(1, 0)
        for h in (0, 1):
            g["up", h].wait_recv()
            if h == 0:
                g["far", 0] = send(dst(below, 0), dst(below, 0), at_f(1, 0))
            g["pup", h] = send(dst(below, h), dst(below, h), at_f(0, 1))
            g["down", 1 - h].wait_recv()
            if h == 0:
                g["far", 1] = send(dst(above, 1), dst(above, 1), at_f(ny - 1, 0))
            g["pdown", 1 - h] = send(dst(above, 1 - h), dst(above, 1 - h), at_f(0, 1))

    def gather_far(g, dst):
        far = feat_of(2, 0)
        for h in (0, 1):
            g["far", h].wait_recv()
            g["pfar", h] = send(dst(far, h), dst(far, h), at_f(0, 1))

    def gather_finish(g):
        for h in (0, 1):
            for name in ("own", "pup", "pdown", "pfar"):
                g[name, h].wait_recv()

    loads[0].wait()
    loads[5].wait()
    lane = iota((8, images), 1)

    def look_up(i, found):
        for k in range(8):
            j = i * 8 + k
            found = jnp.where(lane == j, slot_table[labels[j]], found)
        return found

    found = lax.fori_loop(0, images // 8, look_up, jnp.zeros((8, images), jnp.int32))
    pos_row = jnp.broadcast_to(found[:1].astype(F32), (images, images))
    pos_col = pos_row.T
    own_row = jnp.floor((pos_row + 0.5) * (1.0 / cls_dev))
    own_col = jnp.floor((pos_col + 0.5) * (1.0 / cls_dev))
    ahead = (own_row == own_col) & (iota((images, images), 0) < iota((images, images), 1))
    rank = jnp.sum(jnp.where(ahead, 1.0, 0.0), axis=0, keepdims=True)
    slot = own_row[:1] * cap + rank
    select = (iota((slots, images), 0).astype(F32) == slot).astype(F32).astype(BF16)
    tag = pos_col - own_col * cls_dev + 1.0
    tag_hi = jnp.floor(tag * (1.0 / 32.0))
    lane = iota((images, part), 1)
    tags = jnp.where(lane == 0, tag_hi, jnp.where(lane == 1, tag - 32.0 * tag_hi, 0.0)).astype(BF16)
    loads[1].wait()
    loads[2].wait()
    is_tag = (jnp.zeros((images, part), jnp.int32) + feat) >= full_parts
    wide = jnp.where(is_tag, tags, s_part[...])
    out_w[...] = dot(select, wide).astype(BF16).reshape(out_w.shape)
    out_t[...] = dot(select, t_part[...]).astype(BF16).reshape(out_t.shape)

    pl.semaphore_wait(barrier, len(peers))

    z_copies = {"t": [], "w": []}
    for o in z_order:
        z_copies["t"].append(send(out_t.at[(z + o) % nz], in_t.at[o], at_z(o)))
        z_copies["w"].append(send(out_w.at[(z + o) % nz], in_w.at[o], at_z(o)))
    in_t[0] = out_t[z]
    in_w[0] = out_w[z]

    h_half = d_s // 2

    def h_src(h):
        return head_hbm.at[pl.ds(h * h_half, h_half), :]

    def h_dst(f, h):
        return h_all.at[pl.ds(h * h_half, h_half), pl.ds(pl.multiple_of(f * part, part), part)]

    h_gather = gather_start(h_src, h_dst)
    loads[3].wait()
    n_feat = ny * NC
    q = iota((part, part), 0)
    k = iota((part, part), 1)
    e2 = d_t // (nz * NX * n_feat)
    group = part // n_feat
    by_feat = (q % group) // e2 * (n_feat * e2) + (q // group) * e2 + q % e2
    by_feat = (by_feat == k).astype(F32).astype(BF16)
    by_x = (q % (nz * e2)) // e2 * (NX * e2) + (q // (nz * e2)) * e2 + q % e2
    by_x = (by_x == k).astype(F32).astype(BF16)
    for b in range(d_t // part):
        moved = dot(by_feat, freqs[b * part : (b + 1) * part, :]).astype(BF16)
        f_mid[:, b * group : (b + 1) * group, :] = moved.reshape(n_feat, group, half)
    for f in range(n_feat):
        f_rows[f] = dot(by_x, f_mid[f]).astype(BF16)
    f_copies = [
        send(f_rows.at[j * NC + (1 - c)], f_pair.at[j], at_f(0, 1)) for j in range(ny)
    ]
    q = iota((slots, slots), 0)
    src_row = (q % xrow) // cap * (NX * cap) + (q // xrow) * cap + q % cap
    regroup = (src_row == iota((slots, slots), 1)).astype(F32).astype(BF16)

    gather_near(h_gather, h_dst)

    chunks = {}
    for name, into, out, got in (("t", in_t, xo_t, t_all), ("w", in_w, xo_w, w_all)):
        for copy in z_copies[name]:
            copy.wait_recv()
        moved = dot(regroup, into[...].reshape(slots, part))
        out[...] = moved.astype(BF16).reshape(out.shape)
        chunks[name] = {
            (ox, dy): send(
                out.at[(x + ox) % NX], got.at[pl.ds(ox * xrow, xrow), pl.ds(f_at, part)], at_xy(ox, dy)
            )
            for ox, dy in plane
        }
        got[0:xrow, pl.ds(f_at, part)] = out[x]
    gather_far(h_gather, h_dst)
    forwards = {}
    for name, got in (("t", t_all), ("w", w_all)):
        forwards[name] = []
        for dy in (0, 1, 3, 2):
            for ox in range(NX):
                if (ox, dy) != (0, 0):
                    chunks[name][ox, dy].wait_recv()
            lanes = pl.ds(pl.multiple_of(feat_of(ny - dy, 0) * part, part), part)
            forwards[name].append(send(got.at[:, lanes], got.at[:, lanes], at_f(0, 1)))
    gather_finish(h_gather)
    loads[4].wait()
    for copy in forwards["t"]:
        copy.wait_recv()
    zt_ref[...] = dot(t_all[...], freqs[...])

    block = 32

    def trig_t(i, _):
        r = pl.ds(pl.multiple_of(i * block, block), block)
        zt = zt_ref[r, :]
        cost_ref[r, :] = jnp.cos(zt)
        sint_ref[r, :] = jnp.sin(zt)
        return 0

    lax.fori_loop(0, slots // block, trig_t, 0)
    for copy in forwards["w"]:
        copy.wait_recv()
    for n in range(d_t // half):
        cols = slice(n * half, (n + 1) * half)
        projected = dot(w_all[:, :d_s], h_all[:, cols]).astype(BF16)
        product = dot(projected, freqs[cols, :])
        if n == 0:
            zs_ref[...] = product
        else:
            zs_ref[...] += product

    def trig(i, _):
        r = pl.ds(pl.multiple_of(i * block, block), block)
        zs = zs_ref[r, :]
        sin_s, cos_s = jnp.sin(zs), jnp.cos(zs)
        sin_ref[r, :] = sin_s
        cos_ref[r, :] = cos_s
        upper, lower = split_parts(cos_s - cost_ref[r, :])
        du_ref[r, :half] = upper
        dl_ref[r, :half] = lower
        upper, lower = split_parts(sin_s - sint_ref[r, :])
        du_ref[r, half:] = upper
        dl_ref[r, half:] = lower
        return 0

    lax.fori_loop(0, slots // block, trig, 0)

    tag_block = w_all[:, d_s : d_s + part]
    weight = jnp.where(iota((16, part), 1) == 0, 32.0, jnp.where(iota((16, part), 1) == 1, 1.0, 0.0))
    tag_row = dot(weight.astype(BF16), tag_block, 1, 1)[:1]
    tag_col = tag_block[:, 0:1].astype(F32) * 32.0 + tag_block[:, 1:2].astype(F32)
    alike = jnp.where((tag_row == tag_col) & (tag_col > 0.5), 1.0, 0.0)
    count = jnp.maximum(jnp.sum(alike, axis=1, keepdims=True), 1.0)
    member = alike.astype(BF16)
    sums_cos = dot(member, du_ref[:, :half]) + dot(member, dl_ref[:, :half])
    sums_sin = dot(member, du_ref[:, half:]) + dot(member, dl_ref[:, half:])
    grad_z = (-sin_ref[...] * sums_cos + cos_ref[...] * sums_sin) / count
    grad_z = grad_z.astype(BF16)

    gz_out[...] = grad_z
    gz_copy = send(gz_out, gz_in, at_f(0, 1))
    y_order = (2, 1, 3, 0)
    for dy in y_order:
        u_own[dy] = dot(grad_z, f_rows[feat_of(dy, 0)], 1, 1)
    for copy in f_copies:
        copy.wait_recv()
    gz_copy.wait_recv()
    y_copies = {}
    for dy in y_order[:-1]:
        v_out[dy] = (u_own[dy] + dot(gz_in[...], f_pair[(y + dy) % ny], 1, 1)).astype(BF16)
        y_copies[dy] = send(v_out.at[dy], v_in.at[dy], at_f(dy, 0))
    u_own[0] += dot(gz_in[...], f_pair[y], 1, 1)

    norm = jnp.sum(sums_cos * sums_cos + sums_sin * sums_sin, axis=1, keepdims=True) / count
    wide_cls = loss_out.shape[1]
    holds = (iota((slots, wide_cls), 1).astype(F32) + 1.0) == tag_col
    per_class = jnp.sum(jnp.where(holds, norm, 0.0), axis=0, keepdims=True)
    counts = jnp.maximum(jnp.sum(jnp.where(holds, 1.0, 0.0), axis=0, keepdims=True), 1.0)
    cl_out[0] = per_class / counts * (1.0 / (2.0 * half * n_feat))
    pair = send(cl_out.at[0], cl_in.at[0], at_f(0, 1))

    grad_u = u_own[0]
    for dy in y_order[:-1]:
        y_copies[dy].wait_recv()
        grad_u += v_in[dy].astype(F32)
    u_upper, u_lower = split_parts(grad_u)
    student_in = w_all[:, :d_s]
    partial = dot(u_upper, student_in, 0, 0) + dot(u_lower, student_in, 0, 0)
    hg_ref[...] = partial.reshape(hg_ref.shape)
    hx_out[...] = partial.astype(BF16).reshape(hx_out.shape)
    x_copies = [send(hx_out.at[(x + o) % NX], hx_in.at[o], at_x(o)) for o in (2, 1, 3)]
    total = hg_ref[x]
    pair.wait_recv()
    cl_out[1] = cl_out[0] + cl_in[0]
    c_copies = [send(cl_out.at[1], cl_in.at[dy], at_f(dy, 0)) for dy in range(1, ny)]
    for copy in x_copies:
        copy.wait_recv()
    for o in range(1, NX):
        total += hx_in[o].astype(F32)
    for j in range(nz):
        hz_out[j] = total[j * e2 : (j + 1) * e2, :]
    z_copies = [send(hz_out.at[(z + o) % nz], hz_in.at[o], at_z(o)) for o in z_order]
    hz_in[0] = hz_out[z]
    for copy in c_copies:
        copy.wait_recv()
    loss = cl_out[1]
    for dy in range(1, ny):
        loss += cl_in[dy]
    loss_out[...] = loss
    for copy in z_copies:
        copy.wait_recv()
    grad_out[...] = jnp.sum(hz_in[...], axis=0) * scale
    for copy in started:
        copy.wait_send()


def on_device(teacher, student, head, freqs, labels, class_slot):
    n_dp = lax.axis_size("dp")
    n_feat = lax.axis_size("feat")
    images, d_t = teacher.shape
    d_s = student.shape[1]
    half = freqs.shape[1]
    cls_dev = class_slot.shape[0] // n_dp
    nz = n_dp // NX
    cap = 2 * images // n_dp
    slots = n_dp * cap
    part = d_t // n_feat
    rows_dev = d_t // (n_dp * n_feat)
    wide_cls = -(-cls_dev // 128) * 128
    vmem = pl.BlockSpec(memory_space=pltpu.VMEM)
    hbm = pl.BlockSpec(memory_space=pltpu.HBM)
    scratch = [
        pltpu.VMEM((images, part), BF16),
        pltpu.VMEM((images, part), BF16),
        pltpu.VMEM((d_t, half), BF16),
        pltpu.SMEM(class_slot.shape, jnp.int32),
        pltpu.SMEM(labels.shape, jnp.int32),
        pltpu.VMEM((nz, NX * cap, part), BF16),
        pltpu.VMEM((nz, NX * cap, part), BF16),
        pltpu.VMEM((nz, NX * cap, part), BF16),
        pltpu.VMEM((nz, NX * cap, part), BF16),
        pltpu.VMEM((NX, slots // NX, part), BF16),
        pltpu.VMEM((NX, slots // NX, part), BF16),
        pltpu.VMEM((slots, d_t), BF16),
        pltpu.VMEM((slots, d_t), BF16),
        pltpu.VMEM((d_s, d_t), BF16),
        pltpu.VMEM((n_feat, part, half), BF16),
        pltpu.VMEM((n_feat, part, half), BF16),
        pltpu.VMEM((n_feat // NC, part, half), BF16),
        pltpu.VMEM((slots, half), F32),
        pltpu.VMEM((slots, half), F32),
        pltpu.VMEM((slots, half), F32),
        pltpu.VMEM((slots, half), F32),
        pltpu.VMEM((slots, half), F32),
        pltpu.VMEM((slots, half), F32),
        pltpu.VMEM((slots, 2 * half), BF16),
        pltpu.VMEM((slots, 2 * half), BF16),
        pltpu.VMEM((slots, half), BF16),
        pltpu.VMEM((slots, half), BF16),
        pltpu.VMEM((n_feat // NC, slots, part), F32),
        pltpu.VMEM((n_feat // NC, slots, part), BF16),
        pltpu.VMEM((n_feat // NC, slots, part), BF16),
        pltpu.VMEM((NX, part // NX, d_s), F32),
        pltpu.VMEM((NX, part // NX, d_s), BF16),
        pltpu.VMEM((NX, part // NX, d_s), BF16),
        pltpu.VMEM((nz, rows_dev, d_s), F32),
        pltpu.VMEM((nz, rows_dev, d_s), F32),
        pltpu.VMEM((2, 1, wide_cls), F32),
        pltpu.VMEM((n_feat // NC, 1, wide_cls), F32),
        pltpu.SemaphoreType.DMA((COPIES,)),
        pltpu.SemaphoreType.DMA((COPIES,)),
        pltpu.SemaphoreType.DMA((6,)),
    ]
    grad, loss = pl.pallas_call(
        functools.partial(kernel, cls_dev, 1.0 / math.sqrt(images * n_dp)),
        out_shape=(
            jax.ShapeDtypeStruct((rows_dev, d_s), F32),
            jax.ShapeDtypeStruct((1, wide_cls), F32),
        ),
        in_specs=[hbm] * 6,
        out_specs=(vmem, vmem),
        scratch_shapes=scratch,
        compiler_params=pltpu.CompilerParams(
            collective_id=0, has_side_effects=True, vmem_limit_bytes=66_900_000
        ),
    )(teacher, student, head, freqs, labels, class_slot)
    return (grad, loss[0, :cls_dev])


def solution(mesh):
    in_specs = (P("dp", None), P("dp", None), P(None, "feat"), P(None, "feat"), P("dp"), P())
    out_specs = (P(("dp", "feat"), None), P("dp"))
    return jax.shard_map(
        on_device, mesh=mesh, in_specs=in_specs, out_specs=out_specs, check_vma=False
    )
```

```python
import functools
import math

import jax
import jax.numpy as jnp
from jax import lax
from jax.experimental import pallas as pl
from jax.experimental.pallas import tpu as pltpu
from jax.sharding import PartitionSpec as P

F32, BF16 = jnp.float32, jnp.bfloat16
NX, NC = 4, 2
COPIES = 120


def split_parts(values):
    upper = values.astype(BF16)
    lower = (values - upper.astype(F32)).astype(BF16)
    return (upper, lower)


def dot(a, b, ca=1, cb=0):
    return lax.dot_general(a, b, (((ca,), (cb,)), ((), ())), preferred_element_type=F32)


def iota(shape, axis):
    return lax.broadcasted_iota(jnp.int32, shape, axis)


def kernel(
    cls_dev, scale,
    teacher_hbm, student_hbm, head_hbm, freqs_hbm, labels_hbm, slot_hbm,
    grad_out, loss_out,
    t_part, s_part, freqs, slot_table, labels,
    out_w, out_t, in_w, in_t, xo_w, xo_t, t_all, w_all, h_all, f_mid, f_rows, f_pair,
    zs_ref, zt_ref, cost_ref, sint_ref, sin_ref, cos_ref, du_ref, dl_ref, gz_out, gz_in, u_own, v_out, v_in,
    hg_ref, hx_out, hx_in, hz_own, hz_out, hz_in, cl_out, cl_in, send_sem, recv_sem, load_sem,
):
    dp = lax.axis_index("dp")
    feat = lax.axis_index("feat")
    nz = lax.axis_size("dp") // NX
    ny = lax.axis_size("feat") // NC
    z, x = dp // NX, dp % NX
    y, c = feat // NC, feat % NC
    images, d_t = teacher_hbm.shape
    d_s = student_hbm.shape[1]
    half = freqs_hbm.shape[1]
    cap = 2 * images // (nz * NX)
    slots = nz * NX * cap
    part = d_t // (ny * NC)
    xrow = slots // NX

    def at_z(o):
        return {"dp": ((z + o) % nz) * NX + x, "feat": feat}

    def at_x(o):
        return {"dp": z * NX + (x + o) % NX, "feat": feat}

    def feat_of(dy, dc):
        return ((y + dy) % ny) * NC + (c + dc) % NC

    def at_f(dy, dc):
        return {"dp": dp, "feat": feat_of(dy, dc)}

    def at_xy(ox, dy):
        return {"dp": z * NX + (x + ox) % NX, "feat": feat_of(dy, 0)}

    def hops(o, n):
        return min(o, n - o)

    y_order = (2, 1, 3, 0)
    plane = [(ox, dy) for dy in y_order for ox in (2, 1, 3, 0) if (ox, dy) != (0, 0)]
    z_order = sorted(range(1, nz), key=lambda o: -min(o, nz - o))

    barrier = pltpu.get_barrier_semaphore()
    peers = [at_z(o) for o in z_order] + [at_xy(*p) for p in plane] + [at_f(0, 1)]
    for peer in peers:
        pl.semaphore_signal(barrier, inc=1, device_id=peer, device_id_type=pl.DeviceIdType.MESH)

    f_at = pl.multiple_of(feat * part, part)
    full_parts = d_s // part
    s_at = pl.multiple_of(jnp.minimum(feat, full_parts - 1) * part, part)
    loads = [
        pltpu.make_async_copy(src, dst, load_sem.at[k])
        for k, (src, dst) in enumerate(
            [
                (slot_hbm, slot_table),
                (teacher_hbm.at[:, pl.ds(f_at, part)], t_part),
                (student_hbm.at[:, pl.ds(s_at, part)], s_part),
                (freqs_hbm, freqs),
                (head_hbm, h_all.at[:, pl.ds(f_at, part)]),
                (labels_hbm, labels),
            ]
        )
    ]
    for load in loads:
        load.start()

    started = []

    def send(src, dst, peer):
        k = len(started)
        copy = pltpu.make_async_remote_copy(
            src_ref=src,
            dst_ref=dst,
            send_sem=send_sem.at[k],
            recv_sem=recv_sem.at[k],
            device_id=peer,
            device_id_type=pl.DeviceIdType.MESH,
        )
        copy.start()
        started.append(copy)
        return copy

    def gather_start(src, dst):
        g = {}
        for h in (0, 1):
            g["up", h] = send(src(h), dst(feat, h), at_f(1, 0))
            g["down", 1 - h] = send(src(1 - h), dst(feat, 1 - h), at_f(ny - 1, 0))
        for h in (0, 1):
            g["own", h] = send(src(h), dst(feat, h), at_f(0, 1))
        return g

    def gather_near(g, dst):
        below, above = feat_of(ny - 1, 0), feat_of(1, 0)
        for h in (0, 1):
            g["up", h].wait_recv()
            if h == 0:
                g["far", 0] = send(dst(below, 0), dst(below, 0), at_f(1, 0))
            g["pup", h] = send(dst(below, h), dst(below, h), at_f(0, 1))
            g["down", 1 - h].wait_recv()
            if h == 0:
                g["far", 1] = send(dst(above, 1), dst(above, 1), at_f(ny - 1, 0))
            g["pdown", 1 - h] = send(dst(above, 1 - h), dst(above, 1 - h), at_f(0, 1))

    def gather_far(g, dst):
        far = feat_of(2, 0)
        for h in (0, 1):
            g["far", h].wait_recv()
            g["pfar", h] = send(dst(far, h), dst(far, h), at_f(0, 1))

    def gather_finish(g):
        for h in (0, 1):
            for name in ("own", "pup", "pdown", "pfar"):
                g[name, h].wait_recv()

    loads[0].wait()
    loads[5].wait()
    lane = iota((8, images), 1)

    def look_up(i, found):
        for k in range(8):
            j = i * 8 + k
            found = jnp.where(lane == j, slot_table[labels[j]], found)
        return found

    found = lax.fori_loop(0, images // 8, look_up, jnp.zeros((8, images), jnp.int32))
    pos_row = jnp.broadcast_to(found[:1].astype(F32), (images, images))
    pos_col = pos_row.T
    own_row = jnp.floor((pos_row + 0.5) * (1.0 / cls_dev))
    own_col = jnp.floor((pos_col + 0.5) * (1.0 / cls_dev))
    ahead = (own_row == own_col) & (iota((images, images), 0) < iota((images, images), 1))
    rank = jnp.sum(jnp.where(ahead, 1.0, 0.0), axis=0, keepdims=True)
    slot = own_row[:1] * cap + rank
    select = (iota((slots, images), 0).astype(F32) == slot).astype(F32).astype(BF16)
    tag = pos_col - own_col * cls_dev + 1.0
    tag_hi = jnp.floor(tag * (1.0 / 32.0))
    lane = iota((images, part), 1)
    tags = jnp.where(lane == 0, tag_hi, jnp.where(lane == 1, tag - 32.0 * tag_hi, 0.0)).astype(BF16)
    loads[1].wait()
    loads[2].wait()
    is_tag = (jnp.zeros((images, part), jnp.int32) + feat) >= full_parts
    wide = jnp.where(is_tag, tags, s_part[...])
    out_w[...] = dot(select, wide).astype(BF16).reshape(out_w.shape)
    out_t[...] = dot(select, t_part[...]).astype(BF16).reshape(out_t.shape)

    pl.semaphore_wait(barrier, len(peers))

    z_copies = {"t": [], "w": []}
    z_sends = [("t", out_t, in_t, o, hops(o, nz)) for o in z_order]
    z_sends += [("w", out_w, in_w, o, hops(o, nz) - 2.5) for o in z_order]
    for name, out, into, o, _ in sorted(z_sends, key=lambda e: -e[4]):
        z_copies[name].append(send(out.at[(z + o) % nz], into.at[o], at_z(o)))
    in_t[0] = out_t[z]
    in_w[0] = out_w[z]

    h_half = d_s // 2

    def h_src(h):
        return head_hbm.at[pl.ds(h * h_half, h_half), :]

    def h_dst(f, h):
        return h_all.at[pl.ds(h * h_half, h_half), pl.ds(pl.multiple_of(f * part, part), part)]

    h_gather = gather_start(h_src, h_dst)
    loads[3].wait()
    n_feat = ny * NC
    q = iota((part, part), 0)
    k = iota((part, part), 1)
    e2 = d_t // (nz * NX * n_feat)
    group = part // n_feat
    by_feat = (q % group) // e2 * (n_feat * e2) + (q // group) * e2 + q % e2
    by_feat = (by_feat == k).astype(F32).astype(BF16)
    by_x = (q % (nz * e2)) // e2 * (NX * e2) + (q // (nz * e2)) * e2 + q % e2
    by_x = (by_x == k).astype(F32).astype(BF16)
    for b in range(d_t // part):
        moved = dot(by_feat, freqs[b * part : (b + 1) * part, :]).astype(BF16)
        f_mid[:, b * group : (b + 1) * group, :] = moved.reshape(n_feat, group, half)
    for f in range(n_feat):
        f_rows[f] = dot(by_x, f_mid[f]).astype(BF16)
    f_copies = [
        send(f_rows.at[j * NC + (1 - c)], f_pair.at[j], at_f(0, 1)) for j in range(ny)
    ]
    q = iota((slots, slots), 0)
    src_row = (q % xrow) // cap * (NX * cap) + (q // xrow) * cap + q % cap
    regroup = (src_row == iota((slots, slots), 1)).astype(F32).astype(BF16)

    gather_near(h_gather, h_dst)

    chunks = {}
    for name, into, out, got in (("t", in_t, xo_t, t_all), ("w", in_w, xo_w, w_all)):
        for copy in z_copies[name]:
            copy.wait_recv()
        moved = dot(regroup, into[...].reshape(slots, part))
        out[...] = moved.astype(BF16).reshape(out.shape)
        chunks[name] = {
            (ox, dy): send(
                out.at[(x + ox) % NX], got.at[pl.ds(ox * xrow, xrow), pl.ds(f_at, part)], at_xy(ox, dy)
            )
            for ox, dy in plane
        }
        got[0:xrow, pl.ds(f_at, part)] = out[x]
    gather_far(h_gather, h_dst)
    forwards = {}
    for name, got in (("t", t_all), ("w", w_all)):
        forwards[name] = []
        for dy in y_order:
            for ox in range(NX):
                if (ox, dy) != (0, 0):
                    chunks[name][ox, dy].wait_recv()
            lanes = pl.ds(pl.multiple_of(feat_of(ny - dy, 0) * part, part), part)
            forwards[name].append(send(got.at[:, lanes], got.at[:, lanes], at_f(0, 1)))
    gather_finish(h_gather)
    loads[4].wait()
    for copy in forwards["t"]:
        copy.wait_recv()
    zt_ref[...] = dot(t_all[...], freqs[...])

    block = 32

    def trig_t(i, _):
        r = pl.ds(pl.multiple_of(i * block, block), block)
        zt = zt_ref[r, :]
        cost_ref[r, :] = jnp.cos(zt)
        sint_ref[r, :] = jnp.sin(zt)
        return 0

    lax.fori_loop(0, slots // block, trig_t, 0)
    for copy in forwards["w"]:
        copy.wait_recv()
    for n in range(d_t // half):
        cols = slice(n * half, (n + 1) * half)
        projected = dot(w_all[:, :d_s], h_all[:, cols]).astype(BF16)
        product = dot(projected, freqs[cols, :])
        if n == 0:
            zs_ref[...] = product
        else:
            zs_ref[...] += product

    def trig(i, _):
        r = pl.ds(pl.multiple_of(i * block, block), block)
        zs = zs_ref[r, :]
        sin_s, cos_s = jnp.sin(zs), jnp.cos(zs)
        sin_ref[r, :] = sin_s
        cos_ref[r, :] = cos_s
        upper, lower = split_parts(cos_s - cost_ref[r, :])
        du_ref[r, :half] = upper
        dl_ref[r, :half] = lower
        upper, lower = split_parts(sin_s - sint_ref[r, :])
        du_ref[r, half:] = upper
        dl_ref[r, half:] = lower
        return 0

    lax.fori_loop(0, slots // block, trig, 0)

    tag_block = w_all[:, d_s : d_s + part]
    weight = jnp.where(iota((16, part), 1) == 0, 32.0, jnp.where(iota((16, part), 1) == 1, 1.0, 0.0))
    tag_row = dot(weight.astype(BF16), tag_block, 1, 1)[:1]
    tag_col = tag_block[:, 0:1].astype(F32) * 32.0 + tag_block[:, 1:2].astype(F32)
    alike = jnp.where((tag_row == tag_col) & (tag_col > 0.5), 1.0, 0.0)
    count = jnp.maximum(jnp.sum(alike, axis=1, keepdims=True), 1.0)
    member = alike.astype(BF16)
    sums_cos = dot(member, du_ref[:, :half]) + dot(member, dl_ref[:, :half])
    sums_sin = dot(member, du_ref[:, half:]) + dot(member, dl_ref[:, half:])
    grad_z = (-sin_ref[...] * sums_cos + cos_ref[...] * sums_sin) / count
    grad_z = grad_z.astype(BF16)

    gz_out[...] = grad_z
    gz_copy = send(gz_out, gz_in, at_f(0, 1))
    for dy in y_order:
        u_own[dy] = dot(grad_z, f_rows[feat_of(dy, 0)], 1, 1)
    for copy in f_copies:
        copy.wait_recv()
    gz_copy.wait_recv()
    y_copies = {}
    for dy in y_order[:-1]:
        v_out[dy] = (u_own[dy] + dot(gz_in[...], f_pair[(y + dy) % ny], 1, 1)).astype(BF16)
        y_copies[dy] = send(v_out.at[dy], v_in.at[dy], at_f(dy, 0))
    u_own[0] += dot(gz_in[...], f_pair[y], 1, 1)

    norm = jnp.sum(sums_cos * sums_cos + sums_sin * sums_sin, axis=1, keepdims=True) / count
    wide_cls = loss_out.shape[1]
    holds = (iota((slots, wide_cls), 1).astype(F32) + 1.0) == tag_col
    per_class = jnp.sum(jnp.where(holds, norm, 0.0), axis=0, keepdims=True)
    counts = jnp.maximum(jnp.sum(jnp.where(holds, 1.0, 0.0), axis=0, keepdims=True), 1.0)
    cl_out[0] = per_class / counts * (1.0 / (2.0 * half * n_feat))
    pair = send(cl_out.at[0], cl_in.at[0], at_f(0, 1))

    grad_u = u_own[0]
    for dy in y_order[:-1]:
        y_copies[dy].wait_recv()
        grad_u += v_in[dy].astype(F32)
    u_upper, u_lower = split_parts(grad_u)
    student_in = w_all[:, :d_s]
    partial = dot(u_upper, student_in, 0, 0) + dot(u_lower, student_in, 0, 0)
    hg_ref[...] = partial.reshape(hg_ref.shape)
    hx_out[...] = partial.astype(BF16).reshape(hx_out.shape)
    x_copies = [send(hx_out.at[(x + o) % NX], hx_in.at[o], at_x(o)) for o in (2, 1, 3)]
    total = hg_ref[x]
    pair.wait_recv()
    cl_out[1] = cl_out[0] + cl_in[0]
    c_copies = [send(cl_out.at[1], cl_in.at[dy], at_f(dy, 0)) for dy in range(1, ny)]
    for copy in x_copies:
        copy.wait_recv()
    for o in range(1, NX):
        total += hx_in[o].astype(F32)
    hz_own[...] = total.reshape(hz_own.shape)
    hz_out[...] = hz_own[...].astype(BF16)
    z_copies = [send(hz_out.at[(z + o) % nz], hz_in.at[o], at_z(o)) for o in z_order]
    for copy in c_copies:
        copy.wait_recv()
    loss = cl_out[1]
    for dy in range(1, ny):
        loss += cl_in[dy]
    loss_out[...] = loss
    for copy in z_copies:
        copy.wait_recv()
    total = hz_own[z]
    for o in range(1, nz):
        total += hz_in[o].astype(F32)
    grad_out[...] = total * scale
    for copy in started:
        copy.wait_send()


def on_device(teacher, student, head, freqs, labels, class_slot):
    n_dp = lax.axis_size("dp")
    n_feat = lax.axis_size("feat")
    images, d_t = teacher.shape
    d_s = student.shape[1]
    half = freqs.shape[1]
    cls_dev = class_slot.shape[0] // n_dp
    nz = n_dp // NX
    cap = 2 * images // n_dp
    slots = n_dp * cap
    part = d_t // n_feat
    rows_dev = d_t // (n_dp * n_feat)
    wide_cls = -(-cls_dev // 128) * 128
    vmem = pl.BlockSpec(memory_space=pltpu.VMEM)
    hbm = pl.BlockSpec(memory_space=pltpu.HBM)
    scratch = [
        pltpu.VMEM((images, part), BF16),
        pltpu.VMEM((images, part), BF16),
        pltpu.VMEM((d_t, half), BF16),
        pltpu.SMEM(class_slot.shape, jnp.int32),
        pltpu.SMEM(labels.shape, jnp.int32),
        pltpu.VMEM((nz, NX * cap, part), BF16),
        pltpu.VMEM((nz, NX * cap, part), BF16),
        pltpu.VMEM((nz, NX * cap, part), BF16),
        pltpu.VMEM((nz, NX * cap, part), BF16),
        pltpu.VMEM((NX, slots // NX, part), BF16),
        pltpu.VMEM((NX, slots // NX, part), BF16),
        pltpu.VMEM((slots, d_t), BF16),
        pltpu.VMEM((slots, d_t), BF16),
        pltpu.VMEM((d_s, d_t), BF16),
        pltpu.VMEM((n_feat, part, half), BF16),
        pltpu.VMEM((n_feat, part, half), BF16),
        pltpu.VMEM((n_feat // NC, part, half), BF16),
        pltpu.VMEM((slots, half), F32),
        pltpu.VMEM((slots, half), F32),
        pltpu.VMEM((slots, half), F32),
        pltpu.VMEM((slots, half), F32),
        pltpu.VMEM((slots, half), F32),
        pltpu.VMEM((slots, half), F32),
        pltpu.VMEM((slots, 2 * half), BF16),
        pltpu.VMEM((slots, 2 * half), BF16),
        pltpu.VMEM((slots, half), BF16),
        pltpu.VMEM((slots, half), BF16),
        pltpu.VMEM((n_feat // NC, slots, part), F32),
        pltpu.VMEM((n_feat // NC, slots, part), BF16),
        pltpu.VMEM((n_feat // NC, slots, part), BF16),
        pltpu.VMEM((NX, part // NX, d_s), F32),
        pltpu.VMEM((NX, part // NX, d_s), BF16),
        pltpu.VMEM((NX, part // NX, d_s), BF16),
        pltpu.VMEM((nz, rows_dev, d_s), F32),
        pltpu.VMEM((nz, rows_dev, d_s), BF16),
        pltpu.VMEM((nz, rows_dev, d_s), BF16),
        pltpu.VMEM((2, 1, wide_cls), F32),
        pltpu.VMEM((n_feat // NC, 1, wide_cls), F32),
        pltpu.SemaphoreType.DMA((COPIES,)),
        pltpu.SemaphoreType.DMA((COPIES,)),
        pltpu.SemaphoreType.DMA((6,)),
    ]
    grad, loss = pl.pallas_call(
        functools.partial(kernel, cls_dev, 1.0 / math.sqrt(images * n_dp)),
        out_shape=(
            jax.ShapeDtypeStruct((rows_dev, d_s), F32),
            jax.ShapeDtypeStruct((1, wide_cls), F32),
        ),
        in_specs=[hbm] * 6,
        out_specs=(vmem, vmem),
        scratch_shapes=scratch,
        compiler_params=pltpu.CompilerParams(
            collective_id=0, has_side_effects=True, vmem_limit_bytes=66_900_000
        ),
    )(teacher, student, head, freqs, labels, class_slot)
    return (grad, loss[0, :cls_dev])


def solution(mesh):
    in_specs = (P("dp", None), P("dp", None), P(None, "feat"), P(None, "feat"), P("dp"), P())
    out_specs = (P(("dp", "feat"), None), P("dp"))
    return jax.shard_map(
        on_device, mesh=mesh, in_specs=in_specs, out_specs=out_specs, check_vma=False
    )
```

```python
import functools
import math

import jax
import jax.numpy as jnp
from jax import lax
from jax.experimental import pallas as pl
from jax.experimental.pallas import tpu as pltpu
from jax.sharding import PartitionSpec as P

F32, BF16 = jnp.float32, jnp.bfloat16
NX, NC = 4, 2
COPIES = 120


def split_parts(values):
    upper = values.astype(BF16)
    lower = (values - upper.astype(F32)).astype(BF16)
    return (upper, lower)


def dot(a, b, ca=1, cb=0):
    return lax.dot_general(a, b, (((ca,), (cb,)), ((), ())), preferred_element_type=F32)


def iota(shape, axis):
    return lax.broadcasted_iota(jnp.int32, shape, axis)


def kernel(
    cls_dev, scale,
    teacher_hbm, student_hbm, head_hbm, freqs_hbm, labels_hbm, slot_hbm,
    grad_out, loss_out,
    t_part, s_part, freqs, slot_table, labels,
    out_w, out_t, in_w, in_t, xo_w, xo_t, t_all, w_all, h_all, f_mid, f_rows, f_pair,
    member_ref, count_ref, zs_ref, zt_ref, cost_ref, sint_ref, sin_ref, cos_ref, du_ref, dl_ref, gz_out, gz_in, u_own, v_out, v_in,
    hg_ref, hx_out, hx_in, hz_own, hz_out, hz_in, cl_out, cl_in, send_sem, recv_sem, load_sem,
):
    dp = lax.axis_index("dp")
    feat = lax.axis_index("feat")
    nz = lax.axis_size("dp") // NX
    ny = lax.axis_size("feat") // NC
    z, x = dp // NX, dp % NX
    y, c = feat // NC, feat % NC
    images, d_t = teacher_hbm.shape
    d_s = student_hbm.shape[1]
    half = freqs_hbm.shape[1]
    cap = 2 * images // (nz * NX)
    slots = nz * NX * cap
    part = d_t // (ny * NC)
    xrow = slots // NX

    def at_z(o):
        return {"dp": ((z + o) % nz) * NX + x, "feat": feat}

    def at_x(o):
        return {"dp": z * NX + (x + o) % NX, "feat": feat}

    def feat_of(dy, dc):
        return ((y + dy) % ny) * NC + (c + dc) % NC

    def at_f(dy, dc):
        return {"dp": dp, "feat": feat_of(dy, dc)}

    def at_xy(ox, dy):
        return {"dp": z * NX + (x + ox) % NX, "feat": feat_of(dy, 0)}

    def hops(o, n):
        return min(o, n - o)

    y_order = (2, 1, 3, 0)
    plane = [(ox, dy) for dy in y_order for ox in (2, 1, 3, 0) if (ox, dy) != (0, 0)]
    z_order = sorted(range(1, nz), key=lambda o: -min(o, nz - o))

    barrier = pltpu.get_barrier_semaphore()
    peers = [at_z(o) for o in z_order] + [at_xy(*p) for p in plane] + [at_f(0, 1)]
    for peer in peers:
        pl.semaphore_signal(barrier, inc=1, device_id=peer, device_id_type=pl.DeviceIdType.MESH)

    f_at = pl.multiple_of(feat * part, part)
    full_parts = d_s // part
    s_at = pl.multiple_of(jnp.minimum(feat, full_parts - 1) * part, part)
    loads = [
        pltpu.make_async_copy(src, dst, load_sem.at[k])
        for k, (src, dst) in enumerate(
            [
                (slot_hbm, slot_table),
                (teacher_hbm.at[:, pl.ds(f_at, part)], t_part),
                (student_hbm.at[:, pl.ds(s_at, part)], s_part),
                (freqs_hbm, freqs),
                (head_hbm, h_all.at[:, pl.ds(f_at, part)]),
                (labels_hbm, labels),
            ]
        )
    ]
    for load in loads:
        load.start()

    started = []

    def send(src, dst, peer):
        k = len(started)
        copy = pltpu.make_async_remote_copy(
            src_ref=src,
            dst_ref=dst,
            send_sem=send_sem.at[k],
            recv_sem=recv_sem.at[k],
            device_id=peer,
            device_id_type=pl.DeviceIdType.MESH,
        )
        copy.start()
        started.append(copy)
        return copy

    def gather_start(src, dst):
        g = {}
        for h in (0, 1):
            g["up", h] = send(src(h), dst(feat, h), at_f(1, 0))
            g["down", 1 - h] = send(src(1 - h), dst(feat, 1 - h), at_f(ny - 1, 0))
        for h in (0, 1):
            g["own", h] = send(src(h), dst(feat, h), at_f(0, 1))
        return g

    def gather_near(g, dst):
        below, above = feat_of(ny - 1, 0), feat_of(1, 0)
        for h in (0, 1):
            g["up", h].wait_recv()
            if h == 0:
                g["far", 0] = send(dst(below, 0), dst(below, 0), at_f(1, 0))
            g["pup", h] = send(dst(below, h), dst(below, h), at_f(0, 1))
            g["down", 1 - h].wait_recv()
            if h == 0:
                g["far", 1] = send(dst(above, 1), dst(above, 1), at_f(ny - 1, 0))
            g["pdown", 1 - h] = send(dst(above, 1 - h), dst(above, 1 - h), at_f(0, 1))

    def gather_far(g, dst):
        far = feat_of(2, 0)
        for h in (0, 1):
            g["far", h].wait_recv()
            g["pfar", h] = send(dst(far, h), dst(far, h), at_f(0, 1))

    def gather_finish(g):
        for h in (0, 1):
            for name in ("own", "pup", "pdown", "pfar"):
                g[name, h].wait_recv()

    loads[0].wait()
    loads[5].wait()
    lane = iota((8, images), 1)

    def look_up(i, found):
        for k in range(8):
            j = i * 8 + k
            found = jnp.where(lane == j, slot_table[labels[j]], found)
        return found

    found = lax.fori_loop(0, images // 8, look_up, jnp.zeros((8, images), jnp.int32))
    pos_row = jnp.broadcast_to(found[:1].astype(F32), (images, images))
    pos_col = pos_row.T
    own_row = jnp.floor((pos_row + 0.5) * (1.0 / cls_dev))
    own_col = jnp.floor((pos_col + 0.5) * (1.0 / cls_dev))
    ahead = (own_row == own_col) & (iota((images, images), 0) < iota((images, images), 1))
    rank = jnp.sum(jnp.where(ahead, 1.0, 0.0), axis=0, keepdims=True)
    slot = own_row[:1] * cap + rank
    select = (iota((slots, images), 0).astype(F32) == slot).astype(F32).astype(BF16)
    tag = pos_col - own_col * cls_dev + 1.0
    tag_hi = jnp.floor(tag * (1.0 / 32.0))
    lane = iota((images, part), 1)
    tags = jnp.where(lane == 0, tag_hi, jnp.where(lane == 1, tag - 32.0 * tag_hi, 0.0)).astype(BF16)
    loads[1].wait()
    loads[2].wait()
    is_tag = (jnp.zeros((images, part), jnp.int32) + feat) >= full_parts
    wide = jnp.where(is_tag, tags, s_part[...])
    out_w[...] = dot(select, wide).astype(BF16).reshape(out_w.shape)
    out_t[...] = dot(select, t_part[...]).astype(BF16).reshape(out_t.shape)

    pl.semaphore_wait(barrier, len(peers))

    z_copies = {"t": [], "w": []}
    z_sends = [("t", out_t, in_t, o, hops(o, nz)) for o in z_order]
    z_sends += [("w", out_w, in_w, o, hops(o, nz) - 2.5) for o in z_order]
    for name, out, into, o, _ in sorted(z_sends, key=lambda e: -e[4]):
        z_copies[name].append(send(out.at[(z + o) % nz], into.at[o], at_z(o)))
    in_t[0] = out_t[z]
    in_w[0] = out_w[z]

    h_half = d_s // 2

    def h_src(h):
        return head_hbm.at[pl.ds(h * h_half, h_half), :]

    def h_dst(f, h):
        return h_all.at[pl.ds(h * h_half, h_half), pl.ds(pl.multiple_of(f * part, part), part)]

    h_gather = gather_start(h_src, h_dst)
    loads[3].wait()
    n_feat = ny * NC
    q = iota((part, part), 0)
    k = iota((part, part), 1)
    e2 = d_t // (nz * NX * n_feat)
    group = part // n_feat
    by_feat = (q % group) // e2 * (n_feat * e2) + (q // group) * e2 + q % e2
    by_feat = (by_feat == k).astype(F32).astype(BF16)
    by_x = (q % (nz * e2)) // e2 * (NX * e2) + (q // (nz * e2)) * e2 + q % e2
    by_x = (by_x == k).astype(F32).astype(BF16)
    for b in range(d_t // part):
        moved = dot(by_feat, freqs[b * part : (b + 1) * part, :]).astype(BF16)
        f_mid[:, b * group : (b + 1) * group, :] = moved.reshape(n_feat, group, half)
    for f in range(n_feat):
        f_rows[f] = dot(by_x, f_mid[f]).astype(BF16)
    f_copies = [
        send(f_rows.at[j * NC + (1 - c)], f_pair.at[j], at_f(0, 1)) for j in range(ny)
    ]
    q = iota((slots, slots), 0)
    src_row = (q % xrow) // cap * (NX * cap) + (q // xrow) * cap + q % cap
    regroup = (src_row == iota((slots, slots), 1)).astype(F32).astype(BF16)

    gather_near(h_gather, h_dst)

    chunks = {}
    for name, into, out, got in (("t", in_t, xo_t, t_all), ("w", in_w, xo_w, w_all)):
        for copy in z_copies[name]:
            copy.wait_recv()
        moved = dot(regroup, into[...].reshape(slots, part))
        out[...] = moved.astype(BF16).reshape(out.shape)
        chunks[name] = {
            (ox, dy): send(
                out.at[(x + ox) % NX], got.at[pl.ds(ox * xrow, xrow), pl.ds(f_at, part)], at_xy(ox, dy)
            )
            for ox, dy in plane
        }
        got[0:xrow, pl.ds(f_at, part)] = out[x]
    gather_far(h_gather, h_dst)
    forwards = {}
    for name, got in (("t", t_all), ("w", w_all)):
        forwards[name] = []
        for dy in y_order:
            for ox in range(NX):
                if (ox, dy) != (0, 0):
                    chunks[name][ox, dy].wait_recv()
            lanes = pl.ds(pl.multiple_of(feat_of(ny - dy, 0) * part, part), part)
            forwards[name].append(send(got.at[:, lanes], got.at[:, lanes], at_f(0, 1)))
    gather_finish(h_gather)
    loads[4].wait()
    for copy in forwards["t"]:
        copy.wait_recv()
    zt_ref[...] = dot(t_all[...], freqs[...])

    block = 32

    def trig_t(i, _):
        r = pl.ds(pl.multiple_of(i * block, block), block)
        zt = zt_ref[r, :]
        cost_ref[r, :] = jnp.cos(zt)
        sint_ref[r, :] = jnp.sin(zt)
        return 0

    lax.fori_loop(0, slots // block, trig_t, 0)
    for copy in forwards["w"]:
        copy.wait_recv()
    tag_block = w_all[:, d_s : d_s + part]
    weight = jnp.where(iota((16, part), 1) == 0, 32.0, jnp.where(iota((16, part), 1) == 1, 1.0, 0.0))
    tag_row = dot(weight.astype(BF16), tag_block, 1, 1)[:1]
    tag_col = tag_block[:, 0:1].astype(F32) * 32.0 + tag_block[:, 1:2].astype(F32)
    alike = jnp.where((tag_row == tag_col) & (tag_col > 0.5), 1.0, 0.0)
    count = jnp.maximum(jnp.sum(alike, axis=1, keepdims=True), 1.0)
    member_ref[...] = alike.astype(BF16)
    count_ref[...] = jnp.broadcast_to(count, count_ref.shape)
    for n in range(d_t // half):
        cols = slice(n * half, (n + 1) * half)
        projected = dot(w_all[:, :d_s], h_all[:, cols]).astype(BF16)
        product = dot(projected, freqs[cols, :])
        if n == 0:
            zs_ref[...] = product
        else:
            zs_ref[...] += product

    def trig(i, _):
        r = pl.ds(pl.multiple_of(i * block, block), block)
        zs = zs_ref[r, :]
        sin_s, cos_s = jnp.sin(zs), jnp.cos(zs)
        sin_ref[r, :] = sin_s
        cos_ref[r, :] = cos_s
        upper, lower = split_parts(cos_s - cost_ref[r, :])
        du_ref[r, :half] = upper
        dl_ref[r, :half] = lower
        upper, lower = split_parts(sin_s - sint_ref[r, :])
        du_ref[r, half:] = upper
        dl_ref[r, half:] = lower
        return 0

    lax.fori_loop(0, slots // block, trig, 0)

    member, count = member_ref[...], count_ref[...]
    sums_cos = dot(member, du_ref[:, :half]) + dot(member, dl_ref[:, :half])
    sums_sin = dot(member, du_ref[:, half:]) + dot(member, dl_ref[:, half:])
    grad_z = (-sin_ref[...] * sums_cos + cos_ref[...] * sums_sin) / count
    grad_z = grad_z.astype(BF16)

    gz_out[...] = grad_z
    gz_copy = send(gz_out, gz_in, at_f(0, 1))
    for dy in y_order:
        u_own[dy] = dot(grad_z, f_rows[feat_of(dy, 0)], 1, 1)
    for copy in f_copies:
        copy.wait_recv()
    gz_copy.wait_recv()
    y_copies = {}
    for dy in y_order[:-1]:
        v_out[dy] = (u_own[dy] + dot(gz_in[...], f_pair[(y + dy) % ny], 1, 1)).astype(BF16)
        y_copies[dy] = send(v_out.at[dy], v_in.at[dy], at_f(dy, 0))
    u_own[0] += dot(gz_in[...], f_pair[y], 1, 1)

    norm = jnp.sum(sums_cos * sums_cos + sums_sin * sums_sin, axis=1, keepdims=True) / count[:, :1]
    wide_cls = loss_out.shape[1]
    holds = (iota((slots, wide_cls), 1).astype(F32) + 1.0) == tag_col
    per_class = jnp.sum(jnp.where(holds, norm, 0.0), axis=0, keepdims=True)
    counts = jnp.maximum(jnp.sum(jnp.where(holds, 1.0, 0.0), axis=0, keepdims=True), 1.0)
    cl_out[0] = per_class / counts * (1.0 / (2.0 * half * n_feat))
    pair = send(cl_out.at[0], cl_in.at[0], at_f(0, 1))

    grad_u = u_own[0]
    for dy in y_order[:-1]:
        y_copies[dy].wait_recv()
        grad_u += v_in[dy].astype(F32)
    u_upper, u_lower = split_parts(grad_u)
    student_in = w_all[:, :d_s]
    partial = dot(u_upper, student_in, 0, 0) + dot(u_lower, student_in, 0, 0)
    hg_ref[...] = partial.reshape(hg_ref.shape)
    hx_out[...] = partial.astype(BF16).reshape(hx_out.shape)
    x_copies = [send(hx_out.at[(x + o) % NX], hx_in.at[o], at_x(o)) for o in (2, 1, 3)]
    total = hg_ref[x]
    pair.wait_recv()
    cl_out[1] = cl_out[0] + cl_in[0]
    c_copies = [send(cl_out.at[1], cl_in.at[dy], at_f(dy, 0)) for dy in range(1, ny)]
    for copy in x_copies:
        copy.wait_recv()
    for o in range(1, NX):
        total += hx_in[o].astype(F32)
    hz_own[...] = total.reshape(hz_own.shape)
    hz_out[...] = hz_own[...].astype(BF16)
    z_copies = [send(hz_out.at[(z + o) % nz], hz_in.at[o], at_z(o)) for o in z_order]
    for copy in c_copies:
        copy.wait_recv()
    loss = cl_out[1]
    for dy in range(1, ny):
        loss += cl_in[dy]
    loss_out[...] = loss
    for copy in started[: -len(z_copies)]:
        copy.wait_send()
    for copy in z_copies:
        copy.wait_recv()
    total = hz_own[z]
    for o in range(1, nz):
        total += hz_in[o].astype(F32)
    grad_out[...] = total * scale
    for copy in z_copies:
        copy.wait_send()


def on_device(teacher, student, head, freqs, labels, class_slot):
    n_dp = lax.axis_size("dp")
    n_feat = lax.axis_size("feat")
    images, d_t = teacher.shape
    d_s = student.shape[1]
    half = freqs.shape[1]
    cls_dev = class_slot.shape[0] // n_dp
    nz = n_dp // NX
    cap = 2 * images // n_dp
    slots = n_dp * cap
    part = d_t // n_feat
    rows_dev = d_t // (n_dp * n_feat)
    wide_cls = -(-cls_dev // 128) * 128
    vmem = pl.BlockSpec(memory_space=pltpu.VMEM)
    hbm = pl.BlockSpec(memory_space=pltpu.HBM)
    scratch = [
        pltpu.VMEM((images, part), BF16),
        pltpu.VMEM((images, part), BF16),
        pltpu.VMEM((d_t, half), BF16),
        pltpu.SMEM(class_slot.shape, jnp.int32),
        pltpu.SMEM(labels.shape, jnp.int32),
        pltpu.VMEM((nz, NX * cap, part), BF16),
        pltpu.VMEM((nz, NX * cap, part), BF16),
        pltpu.VMEM((nz, NX * cap, part), BF16),
        pltpu.VMEM((nz, NX * cap, part), BF16),
        pltpu.VMEM((NX, slots // NX, part), BF16),
        pltpu.VMEM((NX, slots // NX, part), BF16),
        pltpu.VMEM((slots, d_t), BF16),
        pltpu.VMEM((slots, d_t), BF16),
        pltpu.VMEM((d_s, d_t), BF16),
        pltpu.VMEM((n_feat, part, half), BF16),
        pltpu.VMEM((n_feat, part, half), BF16),
        pltpu.VMEM((n_feat // NC, part, half), BF16),
        pltpu.VMEM((slots, slots), BF16),
        pltpu.VMEM((slots, half), F32),
        pltpu.VMEM((slots, half), F32),
        pltpu.VMEM((slots, half), F32),
        pltpu.VMEM((slots, half), F32),
        pltpu.VMEM((slots, half), F32),
        pltpu.VMEM((slots, half), F32),
        pltpu.VMEM((slots, half), F32),
        pltpu.VMEM((slots, 2 * half), BF16),
        pltpu.VMEM((slots, 2 * half), BF16),
        pltpu.VMEM((slots, half), BF16),
        pltpu.VMEM((slots, half), BF16),
        pltpu.VMEM((n_feat // NC, slots, part), F32),
        pltpu.VMEM((n_feat // NC, slots, part), BF16),
        pltpu.VMEM((n_feat // NC, slots, part), BF16),
        pltpu.VMEM((NX, part // NX, d_s), F32),
        pltpu.VMEM((NX, part // NX, d_s), BF16),
        pltpu.VMEM((NX, part // NX, d_s), BF16),
        pltpu.VMEM((nz, rows_dev, d_s), F32),
        pltpu.VMEM((nz, rows_dev, d_s), BF16),
        pltpu.VMEM((nz, rows_dev, d_s), BF16),
        pltpu.VMEM((2, 1, wide_cls), F32),
        pltpu.VMEM((n_feat // NC, 1, wide_cls), F32),
        pltpu.SemaphoreType.DMA((COPIES,)),
        pltpu.SemaphoreType.DMA((COPIES,)),
        pltpu.SemaphoreType.DMA((6,)),
    ]
    grad, loss = pl.pallas_call(
        functools.partial(kernel, cls_dev, 1.0 / math.sqrt(images * n_dp)),
        out_shape=(
            jax.ShapeDtypeStruct((rows_dev, d_s), F32),
            jax.ShapeDtypeStruct((1, wide_cls), F32),
        ),
        in_specs=[hbm] * 6,
        out_specs=(vmem, vmem),
        scratch_shapes=scratch,
        compiler_params=pltpu.CompilerParams(
            collective_id=0, has_side_effects=True, vmem_limit_bytes=66_900_000
        ),
    )(teacher, student, head, freqs, labels, class_slot)
    return (grad, loss[0, :cls_dev])


def solution(mesh):
    in_specs = (P("dp", None), P("dp", None), P(None, "feat"), P(None, "feat"), P("dp"), P())
    out_specs = (P(("dp", "feat"), None), P("dp"))
    return jax.shard_map(
        on_device, mesh=mesh, in_specs=in_specs, out_specs=out_specs, check_vma=False
    )
```

```python
import functools
import math

import jax
import jax.numpy as jnp
from jax import lax
from jax.experimental import pallas as pl
from jax.experimental.pallas import tpu as pltpu
from jax.sharding import PartitionSpec as P

F32, BF16 = jnp.float32, jnp.bfloat16
NX, NC = 4, 2
COPIES = 120


def split_parts(values):
    upper = values.astype(BF16)
    lower = (values - upper.astype(F32)).astype(BF16)
    return (upper, lower)


def dot(a, b, ca=1, cb=0):
    return lax.dot_general(a, b, (((ca,), (cb,)), ((), ())), preferred_element_type=F32)


def iota(shape, axis):
    return lax.broadcasted_iota(jnp.int32, shape, axis)


def kernel(
    cls_dev, scale,
    teacher_hbm, student_hbm, head_hbm, freqs_hbm, labels_hbm, slot_hbm,
    grad_out, loss_out,
    t_part, s_part, freqs, slot_table, labels,
    out_w, out_t, in_w, in_t, xo_w, xo_t, t_all, w_all, h_all, f_mid, f_rows, f_pair,
    member_ref, count_ref, zs_ref, zt_ref, cost_ref, sint_ref, sin_ref, cos_ref, du_ref, dl_ref, gz_out, gz_in, u_own, v_out, v_in,
    hg_ref, hx_out, hx_in, hz_own, hz_out, hz_in, cl_out, cl_in, send_sem, recv_sem, load_sem,
):
    dp = lax.axis_index("dp")
    feat = lax.axis_index("feat")
    nz = lax.axis_size("dp") // NX
    ny = lax.axis_size("feat") // NC
    z, x = dp // NX, dp % NX
    y, c = feat // NC, feat % NC
    images, d_t = teacher_hbm.shape
    d_s = student_hbm.shape[1]
    half = freqs_hbm.shape[1]
    cap = 2 * images // (nz * NX)
    slots = nz * NX * cap
    part = d_t // (ny * NC)
    xrow = slots // NX

    def at_z(o):
        return {"dp": ((z + o) % nz) * NX + x, "feat": feat}

    def at_x(o):
        return {"dp": z * NX + (x + o) % NX, "feat": feat}

    def feat_of(dy, dc):
        return ((y + dy) % ny) * NC + (c + dc) % NC

    def at_f(dy, dc):
        return {"dp": dp, "feat": feat_of(dy, dc)}

    def at_xy(ox, dy):
        return {"dp": z * NX + (x + ox) % NX, "feat": feat_of(dy, 0)}

    def hops(o, n):
        return min(o, n - o)

    y_order = (2, 1, 3, 0)
    plane = [(ox, dy) for dy in y_order for ox in (2, 1, 3, 0) if (ox, dy) != (0, 0)]
    z_order = sorted(range(1, nz), key=lambda o: -min(o, nz - o))

    barrier = pltpu.get_barrier_semaphore()
    peers = [at_z(o) for o in z_order] + [at_xy(*p) for p in plane] + [at_f(0, 1)]
    for peer in peers:
        pl.semaphore_signal(barrier, inc=1, device_id=peer, device_id_type=pl.DeviceIdType.MESH)

    f_at = pl.multiple_of(feat * part, part)
    full_parts = d_s // part
    s_at = pl.multiple_of(jnp.minimum(feat, full_parts - 1) * part, part)
    loads = [
        pltpu.make_async_copy(src, dst, load_sem.at[k])
        for k, (src, dst) in enumerate(
            [
                (slot_hbm, slot_table),
                (teacher_hbm.at[:, pl.ds(f_at, part)], t_part),
                (student_hbm.at[:, pl.ds(s_at, part)], s_part),
                (freqs_hbm, freqs),
                (head_hbm, h_all.at[:, pl.ds(f_at, part)]),
                (labels_hbm, labels),
            ]
        )
    ]
    for load in loads:
        load.start()

    started = []

    def send(src, dst, peer):
        k = len(started)
        copy = pltpu.make_async_remote_copy(
            src_ref=src,
            dst_ref=dst,
            send_sem=send_sem.at[k],
            recv_sem=recv_sem.at[k],
            device_id=peer,
            device_id_type=pl.DeviceIdType.MESH,
        )
        copy.start()
        started.append(copy)
        return copy

    def gather_start(src, dst):
        g = {}
        for h in (0, 1):
            g["up", h] = send(src(h), dst(feat, h), at_f(1, 0))
            g["down", 1 - h] = send(src(1 - h), dst(feat, 1 - h), at_f(ny - 1, 0))
        for h in (0, 1):
            g["own", h] = send(src(h), dst(feat, h), at_f(0, 1))
        return g

    def gather_near(g, dst):
        below, above = feat_of(ny - 1, 0), feat_of(1, 0)
        for h in (0, 1):
            g["up", h].wait_recv()
            if h == 0:
                g["far", 0] = send(dst(below, 0), dst(below, 0), at_f(1, 0))
            g["pup", h] = send(dst(below, h), dst(below, h), at_f(0, 1))
            g["down", 1 - h].wait_recv()
            if h == 0:
                g["far", 1] = send(dst(above, 1), dst(above, 1), at_f(ny - 1, 0))
            g["pdown", 1 - h] = send(dst(above, 1 - h), dst(above, 1 - h), at_f(0, 1))

    def gather_far(g, dst):
        far = feat_of(2, 0)
        for h in (0, 1):
            g["far", h].wait_recv()
            g["pfar", h] = send(dst(far, h), dst(far, h), at_f(0, 1))

    def gather_finish(g):
        for h in (0, 1):
            for name in ("own", "pup", "pdown", "pfar"):
                g[name, h].wait_recv()

    loads[0].wait()
    loads[5].wait()
    lane = iota((8, images), 1)

    def look_up(i, found):
        for k in range(8):
            j = i * 8 + k
            found = jnp.where(lane == j, slot_table[labels[j]], found)
        return found

    found = lax.fori_loop(0, images // 8, look_up, jnp.zeros((8, images), jnp.int32))
    pos_row = jnp.broadcast_to(found[:1].astype(F32), (images, images))
    pos_col = pos_row.T
    own_row = jnp.floor((pos_row + 0.5) * (1.0 / cls_dev))
    own_col = jnp.floor((pos_col + 0.5) * (1.0 / cls_dev))
    ahead = (own_row == own_col) & (iota((images, images), 0) < iota((images, images), 1))
    rank = jnp.sum(jnp.where(ahead, 1.0, 0.0), axis=0, keepdims=True)
    slot = own_row[:1] * cap + rank
    select = (iota((slots, images), 0).astype(F32) == slot).astype(F32).astype(BF16)
    tag = pos_col - own_col * cls_dev + 1.0
    tag_hi = jnp.floor(tag * (1.0 / 32.0))
    lane = iota((images, part), 1)
    tags = jnp.where(lane == 0, tag_hi, jnp.where(lane == 1, tag - 32.0 * tag_hi, 0.0)).astype(BF16)
    loads[1].wait()
    loads[2].wait()
    is_tag = (jnp.zeros((images, part), jnp.int32) + feat) >= full_parts
    wide = jnp.where(is_tag, tags, s_part[...])
    out_w[...] = dot(select, wide).astype(BF16).reshape(out_w.shape)
    out_t[...] = dot(select, t_part[...]).astype(BF16).reshape(out_t.shape)

    pl.semaphore_wait(barrier, len(peers))

    z_copies = {"t": [], "w": []}
    z_sends = [("t", out_t, in_t, o, hops(o, nz)) for o in z_order]
    z_sends += [("w", out_w, in_w, o, hops(o, nz) - 2.5) for o in z_order]
    for name, out, into, o, _ in sorted(z_sends, key=lambda e: -e[4]):
        z_copies[name].append(send(out.at[(z + o) % nz], into.at[o], at_z(o)))
    in_t[0] = out_t[z]
    in_w[0] = out_w[z]

    h_half = d_s // 2

    def h_src(h):
        return head_hbm.at[pl.ds(h * h_half, h_half), :]

    def h_dst(f, h):
        return h_all.at[pl.ds(h * h_half, h_half), pl.ds(pl.multiple_of(f * part, part), part)]

    h_gather = gather_start(h_src, h_dst)
    loads[3].wait()
    n_feat = ny * NC
    q = iota((part, part), 0)
    k = iota((part, part), 1)
    e2 = d_t // (nz * NX * n_feat)
    group = part // n_feat
    by_feat = (q % group) // e2 * (n_feat * e2) + (q // group) * e2 + q % e2
    by_feat = (by_feat == k).astype(F32).astype(BF16)
    by_x = (q % (nz * e2)) // e2 * (NX * e2) + (q // (nz * e2)) * e2 + q % e2
    by_x = (by_x == k).astype(F32).astype(BF16)
    for b in range(d_t // part):
        moved = dot(by_feat, freqs[b * part : (b + 1) * part, :]).astype(BF16)
        f_mid[:, b * group : (b + 1) * group, :] = moved.reshape(n_feat, group, half)
    for f in range(n_feat):
        f_rows[f] = dot(by_x, f_mid[f]).astype(BF16)
    f_copies = [
        send(f_rows.at[j * NC + (1 - c)], f_pair.at[j], at_f(0, 1)) for j in range(ny)
    ]
    q = iota((slots, slots), 0)
    src_row = (q % xrow) // cap * (NX * cap) + (q // xrow) * cap + q % cap
    regroup = (src_row == iota((slots, slots), 1)).astype(F32).astype(BF16)

    gather_near(h_gather, h_dst)

    chunks = {}
    for name, into, out, got in (("t", in_t, xo_t, t_all), ("w", in_w, xo_w, w_all)):
        for copy in z_copies[name]:
            copy.wait_recv()
        moved = dot(regroup, into[...].reshape(slots, part))
        out[...] = moved.astype(BF16).reshape(out.shape)
        chunks[name] = {
            (ox, dy): send(
                out.at[(x + ox) % NX], got.at[pl.ds(ox * xrow, xrow), pl.ds(f_at, part)], at_xy(ox, dy)
            )
            for ox, dy in plane
        }
        got[0:xrow, pl.ds(f_at, part)] = out[x]
    gather_far(h_gather, h_dst)
    forwards = {}
    for name, got in (("t", t_all), ("w", w_all)):
        forwards[name] = []
        for dy in y_order:
            for ox in range(NX):
                if (ox, dy) != (0, 0):
                    chunks[name][ox, dy].wait_recv()
            lanes = pl.ds(pl.multiple_of(feat_of(ny - dy, 0) * part, part), part)
            forwards[name].append(send(got.at[:, lanes], got.at[:, lanes], at_f(0, 1)))
    gather_finish(h_gather)
    loads[4].wait()
    for copy in forwards["t"]:
        copy.wait_recv()
    zt_ref[...] = dot(t_all[...], freqs[...])

    block = 32

    def trig_t(i, _):
        r = pl.ds(pl.multiple_of(i * block, block), block)
        zt = zt_ref[r, :]
        cost_ref[r, :] = jnp.cos(zt)
        sint_ref[r, :] = jnp.sin(zt)
        return 0

    lax.fori_loop(0, slots // block, trig_t, 0)
    for copy in forwards["w"]:
        copy.wait_recv()
    tag_block = w_all[:, d_s : d_s + part]
    weight = jnp.where(iota((16, part), 1) == 0, 32.0, jnp.where(iota((16, part), 1) == 1, 1.0, 0.0))
    tag_row = dot(weight.astype(BF16), tag_block, 1, 1)[:1]
    tag_col = tag_block[:, 0:1].astype(F32) * 32.0 + tag_block[:, 1:2].astype(F32)
    alike = jnp.where((tag_row == tag_col) & (tag_col > 0.5), 1.0, 0.0)
    count = jnp.maximum(jnp.sum(alike, axis=1, keepdims=True), 1.0)
    member_ref[...] = alike.astype(BF16)
    count_ref[...] = jnp.broadcast_to(count, count_ref.shape)
    for n in range(d_t // half):
        cols = slice(n * half, (n + 1) * half)
        projected = dot(w_all[:, :d_s], h_all[:, cols]).astype(BF16)
        product = dot(projected, freqs[cols, :])
        if n == 0:
            zs_ref[...] = product
        else:
            zs_ref[...] += product

    def trig(i, _):
        r = pl.ds(pl.multiple_of(i * block, block), block)
        zs = zs_ref[r, :]
        sin_s, cos_s = jnp.sin(zs), jnp.cos(zs)
        sin_ref[r, :] = sin_s
        cos_ref[r, :] = cos_s
        upper, lower = split_parts(cos_s - cost_ref[r, :])
        du_ref[r, :half] = upper
        dl_ref[r, :half] = lower
        upper, lower = split_parts(sin_s - sint_ref[r, :])
        du_ref[r, half:] = upper
        dl_ref[r, half:] = lower
        return 0

    lax.fori_loop(0, slots // block, trig, 0)

    member, count = member_ref[...], count_ref[...]
    sums_cos = dot(member, du_ref[:, :half]) + dot(member, dl_ref[:, :half])
    sums_sin = dot(member, du_ref[:, half:]) + dot(member, dl_ref[:, half:])
    grad_z = (-sin_ref[...] * sums_cos + cos_ref[...] * sums_sin) / count
    grad_z = grad_z.astype(BF16)

    gz_out[...] = grad_z
    gz_copy = send(gz_out, gz_in, at_f(0, 1))
    for dy in y_order:
        u_own[dy] = dot(grad_z, f_rows[feat_of(dy, 0)], 1, 1)
    for copy in f_copies:
        copy.wait_recv()
    gz_copy.wait_recv()
    y_copies = {}
    for dy in y_order[:-1]:
        v_out[dy] = (u_own[dy] + dot(gz_in[...], f_pair[(y + dy) % ny], 1, 1)).astype(BF16)
        y_copies[dy] = send(v_out.at[dy], v_in.at[dy], at_f(dy, 0))
    u_own[0] += dot(gz_in[...], f_pair[y], 1, 1)

    norm = jnp.sum(sums_cos * sums_cos + sums_sin * sums_sin, axis=1, keepdims=True) / count[:, :1]
    wide_cls = loss_out.shape[1]
    holds = (iota((slots, wide_cls), 1).astype(F32) + 1.0) == tag_col
    per_class = jnp.sum(jnp.where(holds, norm, 0.0), axis=0, keepdims=True)
    counts = jnp.maximum(jnp.sum(jnp.where(holds, 1.0, 0.0), axis=0, keepdims=True), 1.0)
    cl_out[0] = per_class / counts * (1.0 / (2.0 * half * n_feat))
    pair = send(cl_out.at[0], cl_in.at[0], at_f(0, 1))

    grad_u = u_own[0]
    for dy in y_order[:-1]:
        y_copies[dy].wait_recv()
        grad_u += v_in[dy].astype(F32)
    u_upper, u_lower = split_parts(grad_u)
    student_in = w_all[:, :d_s]
    partial = dot(u_upper, student_in, 0, 0) + dot(u_lower, student_in, 0, 0)
    hg_ref[...] = partial.reshape(hg_ref.shape)
    hx_out[...] = partial.astype(BF16).reshape(hx_out.shape)
    x_copies = [send(hx_out.at[(x + o) % NX], hx_in.at[o], at_x(o)) for o in (2, 1, 3)]
    total = hg_ref[x]
    pair.wait_recv()
    cl_out[1] = cl_out[0] + cl_in[0]
    c_copies = [send(cl_out.at[1], cl_in.at[dy], at_f(dy, 0)) for dy in range(1, ny)]
    for copy in x_copies:
        copy.wait_recv()
    for o in range(1, NX):
        total += hx_in[o].astype(F32)
    hz_own[...] = total.reshape(hz_own.shape)
    hz_out[...] = hz_own[...].astype(BF16)
    z_copies = [send(hz_out.at[(z + o) % nz], hz_in.at[o], at_z(o)) for o in z_order]
    for copy in c_copies:
        copy.wait_recv()
    loss = cl_out[1]
    for dy in range(1, ny):
        loss += cl_in[dy]
    loss_out[...] = loss
    for copy in started[: -len(z_copies)]:
        copy.wait_send()
    for copy in z_copies:
        copy.wait_recv()
    total = hz_own[z]
    for o in range(1, nz):
        total += hz_in[o].astype(F32)
    grad_out[...] = total * scale
    for copy in z_copies:
        copy.wait_send()


def on_device(teacher, student, head, freqs, labels, class_slot):
    n_dp = lax.axis_size("dp")
    n_feat = lax.axis_size("feat")
    images, d_t = teacher.shape
    d_s = student.shape[1]
    half = freqs.shape[1]
    cls_dev = class_slot.shape[0] // n_dp
    nz = n_dp // NX
    cap = 2 * images // n_dp
    slots = n_dp * cap
    part = d_t // n_feat
    rows_dev = d_t // (n_dp * n_feat)
    wide_cls = -(-cls_dev // 128) * 128
    vmem = pl.BlockSpec(memory_space=pltpu.VMEM)
    hbm = pl.BlockSpec(memory_space=pltpu.HBM)
    scratch = [
        pltpu.VMEM((images, part), BF16),
        pltpu.VMEM((images, part), BF16),
        pltpu.VMEM((d_t, half), BF16),
        pltpu.SMEM(class_slot.shape, jnp.int32),
        pltpu.SMEM(labels.shape, jnp.int32),
        pltpu.VMEM((nz, NX * cap, part), BF16),
        pltpu.VMEM((nz, NX * cap, part), BF16),
        pltpu.VMEM((nz, NX * cap, part), BF16),
        pltpu.VMEM((nz, NX * cap, part), BF16),
        pltpu.VMEM((NX, slots // NX, part), BF16),
        pltpu.VMEM((NX, slots // NX, part), BF16),
        pltpu.VMEM((slots, d_t), BF16),
        pltpu.VMEM((slots, d_t), BF16),
        pltpu.VMEM((d_s, d_t), BF16),
        pltpu.VMEM((n_feat, part, half), BF16),
        pltpu.VMEM((n_feat, part, half), BF16),
        pltpu.VMEM((n_feat // NC, part, half), BF16),
        pltpu.VMEM((slots, slots), BF16),
        pltpu.VMEM((slots, half), F32),
        pltpu.VMEM((slots, half), F32),
        pltpu.VMEM((slots, half), F32),
        pltpu.VMEM((slots, half), F32),
        pltpu.VMEM((slots, half), F32),
        pltpu.VMEM((slots, half), F32),
        pltpu.VMEM((slots, half), F32),
        pltpu.VMEM((slots, 2 * half), BF16),
        pltpu.VMEM((slots, 2 * half), BF16),
        pltpu.VMEM((slots, half), BF16),
        pltpu.VMEM((slots, half), BF16),
        pltpu.VMEM((n_feat // NC, slots, part), F32),
        pltpu.VMEM((n_feat // NC, slots, part), BF16),
        pltpu.VMEM((n_feat // NC, slots, part), BF16),
        pltpu.VMEM((NX, part // NX, d_s), F32),
        pltpu.VMEM((NX, part // NX, d_s), BF16),
        pltpu.VMEM((NX, part // NX, d_s), BF16),
        pltpu.VMEM((nz, rows_dev, d_s), F32),
        pltpu.VMEM((nz, rows_dev, d_s), BF16),
        pltpu.VMEM((nz, rows_dev, d_s), BF16),
        pltpu.VMEM((2, 1, wide_cls), F32),
        pltpu.VMEM((n_feat // NC, 1, wide_cls), F32),
        pltpu.SemaphoreType.DMA((COPIES,)),
        pltpu.SemaphoreType.DMA((COPIES,)),
        pltpu.SemaphoreType.DMA((6,)),
    ]
    grad, loss = pl.pallas_call(
        functools.partial(kernel, cls_dev, 1.0 / math.sqrt(images * n_dp)),
        out_shape=(
            jax.ShapeDtypeStruct((rows_dev, d_s), F32),
            jax.ShapeDtypeStruct((1, wide_cls), F32),
        ),
        in_specs=[hbm] * 6,
        out_specs=(vmem, vmem),
        scratch_shapes=scratch,
        compiler_params=pltpu.CompilerParams(
            collective_id=0, has_side_effects=True, vmem_limit_bytes=56_500_000
        ),
    )(teacher, student, head, freqs, labels, class_slot)
    return (grad, loss[0, :cls_dev])


def solution(mesh):
    in_specs = (P("dp", None), P("dp", None), P(None, "feat"), P(None, "feat"), P("dp"), P())
    out_specs = (P(("dp", "feat"), None), P("dp"))
    return jax.shard_map(
        on_device, mesh=mesh, in_specs=in_specs, out_specs=out_specs, check_vma=False
    )
```
